128 devices in a mesh: px: 8 (over y, core), py: 16 (over z, x).
Axes of the slice: x: 4, y: 4, z: 4, core: 2. Of those that a mesh axis runs over, the one named last changes fastest.
Arguments:
- fine_residual: bfloat16 [524288, 256], P(('px', 'py')), may hold values from -6 to 6
- dest_owner: int32 [524288], P(('px', 'py')), may hold values from 0 to 127, as said below
- coarse_slot: int32 [524288], P(('px', 'py')), may hold values from 0 to 511, as said below
- ghost_slot: int32 [512, 32], P(('px', 'py')), may hold values from 0 to 511, as said below
- child_type: int32 [524288], P(('px', 'py')), may hold values from 0 to 7
- restrict_table: bfloat16 [8, 64, 64], replicated, may hold values from -0.75 to 0.75
- inverse_blocks: bfloat16 [65536, 4096], P(('px', 'py')), may hold values from -0.45 to 1.05
- face_table: bfloat16 [6, 64, 64], replicated, may hold values from -0.75 to 0.75
- face_coef: float32 [16], replicated, may hold values from 0.2 to 2
- coef_index: int32 [6, 65536], P(None, ('px', 'py')), may hold values from 0 to 15
- neighbours: int32 [6, 65536], P(None, ('px', 'py')), may hold values from 0 to 65535, as said below
Outputs:
- coarse_solution: float32 [65536, 256], P(('px', 'py'))
- fine_correction: bfloat16 [524288, 256], P(('px', 'py'))
The draws below stay inside these ranges and needn't reach their ends.
Inputs may be any that keep to these rules, and one draw needn't show every extreme that they name: `dest_owner`: the owner is the element's own device or a device one step away along py (same px index) or along px (same py index); every coarse element has exactly 8 fine children, with distinct child_type. `coarse_slot`: for an element whose parent lives on another device the value is below 32. `ghost_slot`: j = 0, 1, 2, 3 stands for the device one lower along py, one higher along py, one lower along px, one higher along px; a device's four lists hold distinct elements; each remote child of a device's coarse element is found in the list toward the child's device, at the row that its coarse_slot names; between two neighbouring devices at most 32 parents have children across, and some pair has exactly 32. `neighbours`: the element across a face lives on the same device or on a device one step away along py or along px, never outside the grid.
All inputs are finite; a program needn't handle non-finite values.
Results may differ from the reference program's by a relative error of at most 0.0073.
Values may be sent and summed in bfloat16 or wider, within the bound.
No kernel may reach another device: no remote copies, remote signals or barrier semaphores. Data moves between devices by JAX's collectives and lax.ppermute only.
A program may use at most 64 MiB of HBM per device.

```python
import math
import jax
import jax.numpy as jnp

DOF = 64
RHS = 4
W = 256
NTYPE = 8
FACES = 6
KINDS = 16
F_DEV = 4096
C_DEV = 512
GHOST = 32
NF = 524288
NC = 65536
N_PX = 8
N_PY = 16
DEVICES = 128


def geometry(key):
    base = jax.random.fold_in(key, 7)
    device_ids = jnp.arange(DEVICES, dtype=jnp.int32)
    permuted = jax.vmap(lambda number: jax.random.permutation(jax.random.fold_in(base, number), C_DEV))(device_ids).astype(jnp.int32)
    shuffle_key = jax.random.fold_in(base, 3)
    shuffles = jax.vmap(lambda number: jax.random.permutation(jax.random.fold_in(shuffle_key, number), F_DEV))(device_ids).astype(jnp.int32)
    lowest = max(1, GHOST // 2)
    ghost_py = jax.random.randint(jax.random.fold_in(base, 5), (N_PX, N_PY), lowest, GHOST + 1, dtype=jnp.int32)
    ghost_px = jax.random.randint(jax.random.fold_in(base, 6), (N_PX, N_PY), lowest, GHOST + 1, dtype=jnp.int32)
    pick_first = jax.random.randint(jax.random.fold_in(base, 8), (), 0, N_PX, dtype=jnp.int32)
    pick_second = jax.random.randint(jax.random.fold_in(base, 9), (), 0, N_PY - 1, dtype=jnp.int32)
    ghost_py = ghost_py.at[pick_first, pick_second].set(GHOST)
    pick_third = jax.random.randint(jax.random.fold_in(base, 10), (), 0, N_PX - 1, dtype=jnp.int32)
    pick_fourth = jax.random.randint(jax.random.fold_in(base, 12), (), 0, N_PY, dtype=jnp.int32)
    ghost_px = ghost_px.at[pick_third, pick_fourth].set(GHOST)
    record = jnp.arange(F_DEV, dtype=jnp.int32)[None, :]
    parent_local = record // 8
    position_kind = record % 8
    group_id = parent_local // GHOST
    rank_id = parent_local % GHOST
    coord_first = (device_ids // N_PY)[:, None]
    coord_second = (device_ids % N_PY)[:, None]
    limit_zero = ghost_py[coord_first, jnp.maximum(coord_second - 1, 0)]
    limit_one = ghost_py[coord_first, coord_second]
    limit_two = ghost_px[jnp.maximum(coord_first - 1, 0), coord_second]
    limit_three = ghost_px[coord_first, coord_second]
    cross_zero = (group_id == 0) & (coord_second > 0) & (rank_id < limit_zero) & (position_kind >= 4)
    cross_one = (group_id == 1) & (coord_second < N_PY - 1) & (rank_id < limit_one) & (position_kind >= 4)
    cross_two = (group_id == 2) & (coord_first > 0) & (rank_id < limit_two) & (position_kind % 2 == 1)
    cross_three = (group_id == 3) & (coord_first < N_PX - 1) & (rank_id < limit_three) & (position_kind % 2 == 1)
    step_size = jnp.where(cross_zero, -1, jnp.where(cross_one, 1, jnp.where(cross_two, -N_PY, jnp.where(cross_three, N_PY, 0)))).astype(jnp.int32)
    owners = (device_ids[:, None] + step_size).astype(jnp.int32)
    remote = step_size != 0
    local_slot = jnp.take_along_axis(permuted, jnp.broadcast_to(parent_local, (DEVICES, F_DEV)), axis=1)
    slots = jnp.where(remote, jnp.broadcast_to(rank_id, (DEVICES, F_DEV)), local_slot).astype(jnp.int32)
    types = jnp.broadcast_to(position_kind, (DEVICES, F_DEV)).astype(jnp.int32)
    owners = jnp.take_along_axis(owners, shuffles, axis=1)
    slots = jnp.take_along_axis(slots, shuffles, axis=1)
    types = jnp.take_along_axis(types, shuffles, axis=1)
    ghost_lists = permuted[:, :4 * GHOST].reshape(DEVICES * 4, GHOST).astype(jnp.int32)
    return (owners.reshape(NF), slots.reshape(NF), types.reshape(NF), ghost_lists)


def draw_dest_owner(key, part):
    return geometry(key)[0]


def draw_coarse_slot(key, part):
    return geometry(key)[1]


def draw_child_type(key, part):
    return geometry(key)[2]


def draw_ghost_slot(key, part):
    return geometry(key)[3]


def draw_inverse_blocks(key, part):
    noise = jnp.clip(jax.random.normal(key, (NC, DOF, DOF), jnp.float32), -6.0, 6.0)
    identity = jnp.eye(DOF, dtype=jnp.float32)
    blocks = 0.6 * identity[None, :, :] + 0.075 * noise
    return blocks.reshape(NC, DOF * DOF).astype(jnp.bfloat16)


def draw_neighbours(key, part):
    cells = jnp.arange(NC, dtype=jnp.int32)
    owners = cells // C_DEV
    coord_first = (owners // N_PY)[None, :]
    coord_second = (owners % N_PY)[None, :]
    face_ids = jnp.arange(FACES, dtype=jnp.int32)[:, None]
    crossing = jax.random.randint(jax.random.fold_in(key, 11), (FACES, NC), 0, 2, dtype=jnp.int32) == 1
    step_second = jnp.where(face_ids == 0, -1, jnp.where(face_ids == 1, 1, 0))
    step_first = jnp.where(face_ids == 2, -1, jnp.where(face_ids == 3, 1, 0))
    inside = (coord_second + step_second >= 0) & (coord_second + step_second < N_PY) & (coord_first + step_first >= 0) & (coord_first + step_first < N_PX)
    moved = crossing & inside
    target = owners[None, :] + jnp.where(moved, step_first * N_PY + step_second, 0)
    slot_pick = jax.random.randint(jax.random.fold_in(key, 12), (FACES, NC), 0, C_DEV, dtype=jnp.int32)
    return (target * C_DEV + slot_pick).astype(jnp.int32)


def place_ends(result, rng, least, high):
    place = [jax.random.randint(jax.random.fold_in(rng, axis), (), 0, length) for axis, length in enumerate(result.shape)]
    widest = result.shape.index(max(result.shape))
    next_to = place[:widest] + [(place[widest] + 1) % result.shape[widest]] + place[widest + 1:]
    return result.at[tuple(place)].set(least).at[tuple(next_to)].set(high)


def shard_levels(own_key, dims, pieces, low, largest):
    gain, own = 1.0, jax.random.fold_in(own_key, 6)
    for axis_at, parts in pieces:
        heights = jnp.exp(jax.random.uniform(jax.random.fold_in(own, axis_at), (parts,), jnp.float32, low / len(pieces), largest / len(pieces)))
        gain = gain * jnp.repeat(heights, dims[axis_at] // parts).reshape([-1 if axis == axis_at else 1 for axis in range(len(dims))])
    return gain


def normal_values(rng, dims, scale, most, split=(), kind=jnp.bfloat16):
    entries = jax.random.normal(rng, dims, jnp.float32) * scale
    if len(split) > 0:
        entries = shard_levels(rng, dims, split, -0.22, 0.18) * entries
    return jnp.clip(entries, min=-most, max=most).astype(kind)


def setup_inputs(seed: int = 0) -> dict:
    arg_keys = jax.random.split(jax.random.key(seed), 12)
    return {
        "fine_residual": normal_values(arg_keys[0], (NF, W), 1.0, 6.0, ((0, 128),)),
        "dest_owner": draw_dest_owner(jax.random.fold_in(arg_keys[11], 71), 0),
        "coarse_slot": draw_coarse_slot(jax.random.fold_in(arg_keys[11], 71), 0),
        "ghost_slot": draw_ghost_slot(jax.random.fold_in(arg_keys[11], 71), 0),
        "child_type": draw_child_type(jax.random.fold_in(arg_keys[11], 71), 0),
        "restrict_table": normal_values(arg_keys[5], (NTYPE, DOF, DOF), DOF ** -0.5, 0.75),
        "inverse_blocks": draw_inverse_blocks(jax.random.fold_in(arg_keys[11], 71), 0),
        "face_table": normal_values(arg_keys[7], (FACES, DOF, DOF), DOF ** -0.5, 0.75),
        "face_coef": jnp.clip(jnp.exp(jax.random.uniform(arg_keys[8], (KINDS,), jnp.float32, math.log(0.2), math.log(2.0))), 0.2, 2.0),
        "coef_index": place_ends(jax.random.randint(arg_keys[9], (FACES, NC), 0, KINDS), jax.random.fold_in(arg_keys[9], 1), 0, KINDS - 1).astype(jnp.int32),
        "neighbours": draw_neighbours(jax.random.fold_in(arg_keys[11], 71), 0),
    }


omega = 0.5


def typed_apply(blocks, child_type, matrices):
    item_count = blocks.shape[0]
    shaped = blocks.reshape(item_count, RHS, DOF).astype(jnp.float32)
    accum = jnp.zeros((item_count, RHS, DOF), jnp.float32)
    for type_id in range(NTYPE):
        product = jnp.einsum("nsj,ij->nsi", shaped, matrices[type_id].astype(jnp.float32))
        accum = accum + jnp.where((child_type == type_id)[:, None, None], product, jnp.float32(0.0))
    return accum.reshape(item_count, W)


def reference(fine_residual, dest_owner, coarse_slot, ghost_slot, child_type, restrict_table, inverse_blocks, face_table, face_coef, coef_index, neighbours):
    own_device = (jnp.arange(NF, dtype=jnp.int32) // F_DEV).astype(jnp.int32)
    offset = (dest_owner - own_device).astype(jnp.int32)
    is_local = offset == 0
    direction = jnp.where(offset == -1, 1, jnp.where(offset == 1, 0, jnp.where(offset < 0, 3, 2))).astype(jnp.int32)
    ghost_row = jnp.where(is_local, 0, coarse_slot).astype(jnp.int32)
    ghost_pick = ghost_slot[(dest_owner * 4 + direction).astype(jnp.int32), ghost_row]
    parent_slot = jnp.where(is_local, coarse_slot, ghost_pick).astype(jnp.int32)
    parent = (dest_owner * C_DEV + parent_slot).astype(jnp.int32)
    contrib = typed_apply(fine_residual, child_type, restrict_table).astype(jnp.bfloat16)
    coarse_rhs = jax.ops.segment_sum(contrib.astype(jnp.float32), parent, num_segments=NC).astype(jnp.bfloat16)
    inverse = inverse_blocks.reshape(NC, DOF, DOF).astype(jnp.float32)
    first_sweep = jnp.einsum("cij,csj->csi", inverse, coarse_rhs.reshape(NC, RHS, DOF).astype(jnp.float32))
    first_sweep = first_sweep.reshape(NC, W).astype(jnp.bfloat16)
    face_scale = face_coef[coef_index]
    coupled = jnp.zeros((NC, RHS, DOF), jnp.float32)
    for face_id in range(FACES):
        beside = first_sweep[neighbours[face_id]].reshape(NC, RHS, DOF).astype(jnp.float32)
        product = jnp.einsum("csj,ij->csi", beside, face_table[face_id].astype(jnp.float32))
        coupled = coupled + face_scale[face_id][:, None, None] * product
    coupled = coupled.astype(jnp.bfloat16)
    correction = jnp.einsum("cij,csj->csi", inverse, coupled.astype(jnp.float32)).reshape(NC, W)
    coarse_solution = first_sweep.astype(jnp.float32) - omega * correction
    answer = coarse_solution.astype(jnp.bfloat16)
    fetched = answer[parent]
    fine_correction = typed_apply(fetched, child_type, jnp.transpose(restrict_table, (0, 2, 1))).astype(jnp.bfloat16)
    return coarse_solution, fine_correction
```

```python
import jax
import jax.numpy as jnp
from jax import lax
from jax.experimental import pallas as pl
from jax.experimental.pallas import tpu as pltpu
from jax.sharding import PartitionSpec as P

bf16 = jnp.bfloat16
f32 = jnp.float32
i32 = jnp.int32

OMEGA = 0.5
DOF = 64
RHS = 4
W = 256
NTYPE = 8
FACES = 6
KINDS = 16
GHOST = 32
LANES = 128
CHUNK = 1024


def swap_pairs(n_px, n_py):
    def at(a, b):
        return (a % n_px) * n_py + b % n_py

    perms = []
    for start in (0, 1):
        perm = []
        for b in range(n_py):
            for a in range(start, n_px + start, 2):
                perm += [(at(a, b), at(a + 1, b)), (at(a + 1, b), at(a, b))]
        perms.append(sorted(perm))
    for start in (0, 1):
        perm = []
        for a in range(n_px):
            for b in range(start, n_py + start, 2):
                perm += [(at(a, b), at(a, b + 1)), (at(a, b + 1), at(a, b))]
        perms.append(sorted(perm))
    return perms


def exchange(arrays, perms):
    return [lax.ppermute(x, ("px", "py"), perm) for x, perm in zip(arrays, perms)]


def wide(column):
    return jnp.concatenate([column, column], axis=1)


def block_diagonal(matrix, flipped):
    row = lax.broadcasted_iota(i32, (W, DOF), 0) % DOF
    col = lax.broadcasted_iota(i32, (W, DOF), 1)
    spread = (row == col).astype(f32).astype(bf16)
    dims = (((1,), (1 if flipped else 0,)), ((), ()))
    half = lax.dot_general(spread, matrix, dims, preferred_element_type=f32).astype(bf16)
    full = lax.dot_general(half, spread, (((1,), (1,)), ((), ())), preferred_element_type=f32)
    r = lax.broadcasted_iota(i32, (W, W), 0) // DOF
    c = lax.broadcasted_iota(i32, (W, W), 1) // DOF
    return jnp.where(r == c, full, 0.0).astype(bf16)


def targets(where_ref, dest, slot, coarse_count):
    own = where_ref[0]
    even_x = where_ref[1]
    even_y = where_ref[2]
    off = dest - own
    q_px = jnp.where((off > 0) == (even_x == 1), 0, 1)
    q_py = jnp.where((off > 0) == (even_y == 1), 2, 3)
    q = jnp.where((off == 1) | (off == -1), q_py, q_px)
    return jnp.where(off == 0, slot, coarse_count + q * GHOST + slot)


def columns(rows):
    flipped = rows.T
    return [jnp.broadcast_to(flipped[:, r : r + 1], (LANES, LANES)) for r in range(rows.shape[0])]


def typed(x_rows, type_column, table):
    kinds = wide(type_column.astype(f32).astype(bf16))
    parts = [jnp.where(kinds == float(t), x_rows, jnp.zeros((), bf16)) for t in range(NTYPE)]
    return jnp.dot(jnp.concatenate(parts, axis=1), table, preferred_element_type=f32)


def restrict_kernel(where_ref, x_ref, dest_ref, slot_ref, type_ref, table_ref, local_ref, g0, g1, g2, g3, w_ref, contrib_ref, acc_ref):
    step = pl.program_id(0)
    rows_out = acc_ref.shape[0]
    coarse_count = rows_out - 4 * GHOST

    @pl.when(step == 0)
    def _():
        for t in range(NTYPE):
            w_ref[t * W : (t + 1) * W, :] = block_diagonal(table_ref[t], True)
        acc_ref[...] = jnp.zeros_like(acc_ref)

    table = w_ref[...]
    kinds = columns(type_ref[...])
    for r in range(CHUNK // LANES):
        rows = slice(r * LANES, (r + 1) * LANES)
        contrib_ref[rows, :] = typed(x_ref[rows, :], kinds[r], table).astype(bf16)
    target = targets(where_ref, dest_ref[...], slot_ref[...], coarse_count)
    row_id = lax.broadcasted_iota(i32, (rows_out, LANES), 0)
    hits = [
        (row_id == jnp.broadcast_to(target[r : r + 1, :], (rows_out, LANES))).astype(f32).astype(bf16)
        for r in range(CHUNK // LANES)
    ]
    acc_ref[...] += jnp.dot(jnp.concatenate(hits, axis=1), contrib_ref[...], preferred_element_type=f32)

    @pl.when(step == pl.num_programs(0) - 1)
    def _():
        local_ref[...] = acc_ref[:coarse_count, :]
        for q, out in enumerate((g0, g1, g2, g3)):
            first = coarse_count + q * GHOST
            out[...] = acc_ref[first : first + GHOST, :].astype(bf16)


def apply_blocks(inv_ref, v):
    count = v.shape[0]
    lane = lax.broadcasted_iota(i32, (count, LANES), 1)
    outs = []
    row = lax.broadcasted_iota(i32, (W, DOF), 0)
    col = lax.broadcasted_iota(i32, (W, DOF), 1)
    doubled = []
    for s in range(RHS):
        tile = v[:, (s // 2) * LANES : (s // 2 + 1) * LANES].astype(f32)
        turned = pltpu.roll(tile, DOF, 1)
        low, high = (tile, turned) if s % 2 == 0 else (turned, tile)
        doubled.append(wide(jnp.where(lane < DOF, low, high).astype(bf16)))
    acc = [jnp.zeros((count, DOF), f32) for _ in range(RHS)]
    for k in range(DOF * DOF // W):
        summing = (col == row // DOF + k * (W // DOF)).astype(f32).astype(bf16)
        block = inv_ref[:, k * W : (k + 1) * W]
        for s in range(RHS):
            acc[s] = acc[s] + jnp.dot(block * doubled[s], summing, preferred_element_type=f32)
    return jnp.concatenate(acc, axis=1)


def sweep_kernel(local_ref, i0, i1, i2, i3, slots_ref, inv_ref, out_ref):
    count = local_ref.shape[0]
    row_id = lax.broadcasted_iota(i32, (count, LANES), 0)
    hits = (row_id == jnp.broadcast_to(slots_ref[0:1, :], (count, LANES))).astype(f32).astype(bf16)
    incoming = jnp.concatenate([i0[...], i1[...], i2[...], i3[...]], axis=0)
    rhs = local_ref[...] + jnp.dot(hits, incoming, preferred_element_type=f32)
    out_ref[...] = apply_blocks(inv_ref, rhs.astype(bf16)).astype(bf16)


def couple_kernel(
    where_ref, fs_ref, h0, h1, h2, h3, nb_ref, ci_ref, coef_ref, face_ref, slots_ref, inv_ref,
    sol_ref, ans_ref, r0, r1, r2, r3,
):
    count = fs_ref.shape[0]
    own = where_ref[0]
    even_x = where_ref[1]
    even_y = where_ref[2]
    nb = nb_ref[...]
    off = nb // count - own
    q_px = jnp.where((off > 0) == (even_x == 1), 1, 2)
    q_py = jnp.where((off > 0) == (even_y == 1), 3, 4)
    block = jnp.where(off == 0, 0, jnp.where((off == 1) | (off == -1), q_py, q_px))
    index = block * count + nb % count
    scale = jnp.zeros(nb.shape, f32)
    for k in range(KINDS):
        scale = jnp.where(ci_ref[...] == k, coef_ref[k], scale)
    index_t = index.T
    scale_t = scale.T
    sources = [fs_ref, h0, h1, h2, h3]
    lane = lax.broadcasted_iota(i32, (count, W), 1)
    coupled = jnp.zeros((count, W), f32)
    for f in range(FACES):
        column = jnp.broadcast_to(index_t[:, f : f + 1], (count, LANES))
        column = wide(column)
        acc = jnp.zeros((count, W), f32)
        for b in range(5):
            for h in range(count // W):
                hit = (lane + (b * count + h * W) == column).astype(f32).astype(bf16)
                acc = acc + jnp.dot(hit, sources[b][h * W : (h + 1) * W, :], preferred_element_type=f32)
        term = jnp.dot(acc.astype(bf16), block_diagonal(face_ref[f], True), preferred_element_type=f32)
        coupled = coupled + term * wide(jnp.broadcast_to(scale_t[:, f : f + 1], (count, LANES)))
    correction = apply_blocks(inv_ref, coupled.astype(bf16))
    solution_rows = fs_ref[...].astype(f32) - OMEGA * correction
    sol_ref[...] = solution_rows
    answer = solution_rows.astype(bf16)
    ans_ref[...] = answer
    row_id = lax.broadcasted_iota(i32, (count, LANES), 0)
    hits = (row_id == jnp.broadcast_to(slots_ref[0:1, :], (count, LANES))).astype(f32).astype(bf16)
    replies = lax.dot_general(hits, answer, (((0,), (0,)), ((), ())), preferred_element_type=f32).astype(bf16)
    for q, out in enumerate((r0, r1, r2, r3)):
        out[...] = replies[q * GHOST : (q + 1) * GHOST, :]


def prolong_kernel(where_ref, ans_ref, r0, r1, r2, r3, dest_ref, slot_ref, type_ref, table_ref, out_ref, w_ref, t_ref):
    step = pl.program_id(0)
    rows_in = t_ref.shape[0]
    coarse_count = rows_in - 4 * GHOST

    @pl.when(step == 0)
    def _():
        for t in range(NTYPE):
            w_ref[t * W : (t + 1) * W, :] = block_diagonal(table_ref[t], False)
        t_ref[:coarse_count, :] = ans_ref[...]
        for q, r in enumerate((r0, r1, r2, r3)):
            first = coarse_count + q * GHOST
            t_ref[first : first + GHOST, :] = r[...]

    table = w_ref[...]
    source = t_ref[...]
    kinds = columns(type_ref[...])
    target = columns(targets(where_ref, dest_ref[...], slot_ref[...], coarse_count))
    lane = lax.broadcasted_iota(i32, (LANES, LANES), 1)
    for r in range(CHUNK // LANES):
        hits = [
            (lane + k * LANES == target[r]).astype(f32).astype(bf16) for k in range(rows_in // LANES)
        ]
        fetched = jnp.dot(jnp.concatenate(hits, axis=1), source, preferred_element_type=f32).astype(bf16)
        out_ref[r * LANES : (r + 1) * LANES, :] = typed(fetched, kinds[r], table).astype(bf16)


def whole(shape):
    return pl.BlockSpec(shape, lambda *_: (0,) * len(shape))


def shards(
    fine_residual, dest_owner, coarse_slot, ghost_slot, child_type, restrict_table, inverse_blocks,
    face_table, face_coef, coef_index, neighbours,
):
    fine_count = fine_residual.shape[0]
    count = inverse_blocks.shape[0]
    n_px, n_py = lax.axis_size("px"), lax.axis_size("py")
    a, b = lax.axis_index("px"), lax.axis_index("py")
    even_x, even_y = 1 - a % 2, 1 - b % 2
    where = jnp.stack([a * n_py + b, even_x, even_y]).astype(i32)
    perms = swap_pairs(n_px, n_py)
    lists = jnp.stack([
        jnp.where(even_x == 1, ghost_slot[3], ghost_slot[2]),
        jnp.where(even_x == 1, ghost_slot[2], ghost_slot[3]),
        jnp.where(even_y == 1, ghost_slot[1], ghost_slot[0]),
        jnp.where(even_y == 1, ghost_slot[0], ghost_slot[1]),
    ]).reshape(1, 4 * GHOST)
    meta = [m.reshape(fine_count // LANES, LANES) for m in (dest_owner, coarse_slot, child_type)]
    steps = fine_count // CHUNK
    smem = pl.BlockSpec(memory_space=pltpu.SMEM)
    meta_spec = pl.BlockSpec((CHUNK // LANES, LANES), lambda i: (i, 0))
    ghost_shape = [jax.ShapeDtypeStruct((GHOST, W), bf16)] * 4
    ghost_spec = [whole((GHOST, W))] * 4
    rows = count + 4 * GHOST

    local, *outgoing = pl.pallas_call(
        restrict_kernel,
        grid=(steps,),
        in_specs=[smem, pl.BlockSpec((CHUNK, W), lambda i: (i, 0)), meta_spec, meta_spec, meta_spec, whole(restrict_table.shape)],
        out_specs=[whole((count, W))] + ghost_spec,
        out_shape=[jax.ShapeDtypeStruct((count, W), f32)] + ghost_shape,
        scratch_shapes=[pltpu.VMEM((NTYPE * W, W), bf16), pltpu.VMEM((CHUNK, W), bf16), pltpu.VMEM((rows, W), f32)],
        name="restrict",
    )(where, fine_residual, *meta, restrict_table)
    incoming = exchange(outgoing, perms)
    first_sweep = pl.pallas_call(
        sweep_kernel,
        out_shape=jax.ShapeDtypeStruct((count, W), bf16),
        name="sweep",
    )(local, *incoming, lists, inverse_blocks)
    halo = exchange([first_sweep] * 4, perms)
    coarse_solution, answer, *replies = pl.pallas_call(
        couple_kernel,
        in_specs=[smem] + [pl.BlockSpec()] * 7 + [smem] + [pl.BlockSpec()] * 3,
        out_shape=[jax.ShapeDtypeStruct((count, W), f32), jax.ShapeDtypeStruct((count, W), bf16)] + ghost_shape,
        name="couple",
    )(where, first_sweep, *halo, neighbours, coef_index, face_coef, face_table, lists, inverse_blocks)
    returned = exchange(replies, perms)
    fine_correction = pl.pallas_call(
        prolong_kernel,
        grid=(steps,),
        in_specs=[smem, whole((count, W))] + ghost_spec + [meta_spec, meta_spec, meta_spec, whole(restrict_table.shape)],
        out_specs=pl.BlockSpec((CHUNK, W), lambda i: (i, 0)),
        out_shape=jax.ShapeDtypeStruct((fine_count, W), bf16),
        scratch_shapes=[pltpu.VMEM((NTYPE * W, W), bf16), pltpu.VMEM((rows, W), bf16)],
        name="prolong",
    )(where, answer, *returned, *meta, restrict_table)
    return (coarse_solution, fine_correction)


def solution(mesh):
    both = ("px", "py")
    in_specs = (
        P(both, None), P(both), P(both), P(both, None), P(both), P(), P(both, None), P(), P(), P(None, both), P(None, both),
    )
    out_specs = (P(both, None), P(both, None))
    return jax.shard_map(shards, mesh=mesh, in_specs=in_specs, out_specs=out_specs, check_vma=False)
```

```python
import jax
import jax.numpy as jnp
from jax import lax
from jax.experimental import pallas as pl
from jax.experimental.pallas import tpu as pltpu
from jax.sharding import PartitionSpec as P


bf16 = jnp.bfloat16
f32 = jnp.float32
i32 = jnp.int32
i16 = jnp.int16

OMEGA = 0.5
DOF = 64
RHS = 4
W = 256
NTYPE = 8
FACES = 6
KINDS = 16
GHOST = 32
LANES = 128
CHUNK = 1024


def swap_pairs(n_px, n_py):
    def at(a, b):
        return (a % n_px) * n_py + b % n_py

    perms = []
    for start in (0, 1):
        perm = []
        for b in range(n_py):
            for a in range(start, n_px + start, 2):
                perm += [(at(a, b), at(a + 1, b)), (at(a + 1, b), at(a, b))]
        perms.append(sorted(perm))
    for start in (0, 1):
        perm = []
        for a in range(n_px):
            for b in range(start, n_py + start, 2):
                perm += [(at(a, b), at(a, b + 1)), (at(a, b + 1), at(a, b))]
        perms.append(sorted(perm))
    return perms


def exchange(arrays, perms):
    moved = []
    for x, perm in zip(arrays, perms):
        moved.append(pltpu.with_memory_space_constraint(lax.ppermute(x, ("px", "py"), perm), pltpu.VMEM))
    return moved


def wide(column):
    return jnp.concatenate([column, column], axis=1)


def block_diagonal(matrix, flipped):
    row = lax.broadcasted_iota(i32, (W, DOF), 0) % DOF
    col = lax.broadcasted_iota(i32, (W, DOF), 1)
    spread = (row == col).astype(f32).astype(bf16)
    dims = (((1,), (1 if flipped else 0,)), ((), ()))
    half = lax.dot_general(spread, matrix, dims, preferred_element_type=f32).astype(bf16)
    full = lax.dot_general(half, spread, (((1,), (1,)), ((), ())), preferred_element_type=f32)
    r = lax.broadcasted_iota(i32, (W, W), 0) // DOF
    c = lax.broadcasted_iota(i32, (W, W), 1) // DOF
    return jnp.where(r == c, full, 0.0).astype(bf16)


def position():
    a, b = lax.axis_index("px"), lax.axis_index("py")
    n_py = lax.axis_size("py")
    return a * n_py + b, lax.rem(a, 2) == 0, lax.rem(b, 2) == 0


def partner(off, even_x, even_y):
    q_px = jnp.where((off > 0) == even_x, 0, 1)
    q_py = jnp.where((off > 0) == even_y, 2, 3)
    return jnp.where((off == 1) | (off == -1), q_py, q_px)


def targets(dest, slot, coarse_count):
    own, even_x, even_y = position()
    off = dest - own
    return jnp.where(off == 0, slot, coarse_count + partner(off, even_x, even_y) * GHOST + slot)


def list_rows(ghost):
    _, even_x, even_y = position()
    low_y, high_y, low_x, high_x = (ghost[j : j + 1, :] for j in range(4))
    ordered = [
        jnp.where(even_x, high_x, low_x),
        jnp.where(even_x, low_x, high_x),
        jnp.where(even_y, high_y, low_y),
        jnp.where(even_y, low_y, high_y),
    ]
    return jnp.broadcast_to(jnp.concatenate(ordered, axis=1), (8, 4 * GHOST))


def ones_where(mask):
    return jnp.where(mask, jnp.ones((), bf16), jnp.zeros((), bf16))


def one_hot_rows(values, row_count):
    row_id = lax.broadcasted_iota(i32, (row_count, LANES), 0).astype(i16)
    hits = []
    for r in range(values.shape[0]):
        wanted = jnp.broadcast_to(values[r : r + 1, :], (16, LANES)).astype(i16)
        wanted = jnp.concatenate([wanted] * (row_count // 16), axis=0)
        hits.append(ones_where(row_id == wanted))
    return jnp.concatenate(hits, axis=1)


def columns(rows):
    flipped = rows.T
    parts = [
        jnp.broadcast_to(flipped[:, r : r + 1], (LANES, LANES)).astype(i16) for r in range(rows.shape[0])
    ]
    return jnp.concatenate(parts, axis=0)


def one_hot_columns(column, row_count):
    lane = lax.broadcasted_iota(i32, column.shape, 1).astype(i16)
    return jnp.concatenate(
        [ones_where(column - jnp.asarray(k * LANES, i16) == lane) for k in range(row_count // LANES)], axis=1
    )


def typed(x_rows, kinds, table):
    kinds = wide(kinds)
    parts = [jnp.where(kinds == jnp.asarray(t, i16), x_rows, jnp.zeros((), bf16)) for t in range(NTYPE)]
    return jnp.dot(jnp.concatenate(parts, axis=1), table, preferred_element_type=f32)


def restrict_kernel(x_ref, dest_ref, slot_ref, type_ref, table_ref, local_ref, g0, g1, g2, g3, w_ref, acc_ref):
    step = pl.program_id(0)
    rows_out = acc_ref.shape[0]
    coarse_count = rows_out - 4 * GHOST

    @pl.when(step == 0)
    def _():
        for t in range(NTYPE):
            w_ref[t * W : (t + 1) * W, :] = block_diagonal(table_ref[t], True)
        acc_ref[...] = jnp.zeros_like(acc_ref)

    contrib = typed(x_ref[...], columns(type_ref[...]), w_ref[...]).astype(bf16)
    hits = one_hot_rows(targets(dest_ref[...], slot_ref[...], coarse_count), rows_out)
    acc_ref[...] += jnp.dot(hits, contrib, preferred_element_type=f32)

    @pl.when(step == pl.num_programs(0) - 1)
    def _():
        local_ref[...] = acc_ref[:coarse_count, :]
        for q, out in enumerate((g0, g1, g2, g3)):
            first = coarse_count + q * GHOST
            out[...] = acc_ref[first : first + GHOST, :].astype(bf16)


def apply_blocks(inv_ref, v):
    count = v.shape[0]
    lane = lax.broadcasted_iota(i32, (count, LANES), 1)
    row = lax.broadcasted_iota(i32, (DOF * DOF, DOF), 0)
    col = lax.broadcasted_iota(i32, (DOF * DOF, DOF), 1)
    summing = (col == row // DOF).astype(f32).astype(bf16)
    outs = []
    for s in range(RHS):
        tile = v[:, (s // 2) * LANES : (s // 2 + 1) * LANES].astype(f32)
        turned = pltpu.roll(tile, DOF, 1)
        low, high = (tile, turned) if s % 2 == 0 else (turned, tile)
        doubled = jnp.where(lane < DOF, low, high).astype(bf16)
        products = jnp.concatenate(
            [inv_ref[:, k * LANES : (k + 1) * LANES] * doubled for k in range(DOF * DOF // LANES)], axis=1
        )
        outs.append(jnp.dot(products, summing, preferred_element_type=f32))
    return jnp.concatenate(outs, axis=1)


def sweep_kernel(local_ref, i0, i1, i2, i3, ghost_ref, inv_ref, out_ref):
    count = local_ref.shape[0]
    hits = one_hot_rows(list_rows(ghost_ref[...])[:1], count)
    incoming = jnp.concatenate([i0[...], i1[...], i2[...], i3[...]], axis=0)
    rhs = local_ref[...] + jnp.dot(hits, incoming, preferred_element_type=f32)
    out_ref[...] = apply_blocks(inv_ref, rhs.astype(bf16)).astype(bf16)


def couple_kernel(
    coef_ref, fs_ref, h0, h1, h2, h3, nb_ref, ci_ref, face_ref, ghost_ref, inv_ref,
    sol_ref, ans_ref, r0, r1, r2, r3, t_ref,
):
    count = fs_ref.shape[0]
    own, even_x, even_y = position()
    nb = nb_ref[...]
    off = nb // count - own
    block = jnp.where(off == 0, 0, 1 + partner(off, even_x, even_y))
    index = block * count + nb % count
    scale = jnp.zeros(nb.shape, f32)
    for k in range(KINDS):
        scale = jnp.where(ci_ref[...] == k, coef_ref[k], scale)
    index_t = index.T
    scale_t = scale.T
    for b, source in enumerate((fs_ref, h0, h1, h2, h3)):
        t_ref[b * count : (b + 1) * count, :] = source[...]
    coupled = jnp.zeros((count, W), f32)
    for f in range(FACES):
        column = jnp.broadcast_to(index_t[:, f : f + 1], (count, LANES)).astype(i16)
        beside = jnp.dot(one_hot_columns(column, 5 * count), t_ref[...], preferred_element_type=f32)
        term = jnp.dot(beside.astype(bf16), block_diagonal(face_ref[f], True), preferred_element_type=f32)
        coupled = coupled + term * wide(jnp.broadcast_to(scale_t[:, f : f + 1], (count, LANES)))
    correction = apply_blocks(inv_ref, coupled.astype(bf16))
    solution_rows = fs_ref[...].astype(f32) - OMEGA * correction
    sol_ref[...] = solution_rows
    answer = solution_rows.astype(bf16)
    ans_ref[...] = answer
    listed = jnp.broadcast_to(list_rows(ghost_ref[...]).T[:, :1], (4 * GHOST, LANES)).astype(i16)
    replies = jnp.dot(one_hot_columns(listed, count), answer, preferred_element_type=f32).astype(bf16)
    for q, out in enumerate((r0, r1, r2, r3)):
        out[...] = replies[q * GHOST : (q + 1) * GHOST, :]


def prolong_kernel(ans_ref, r0, r1, r2, r3, dest_ref, slot_ref, type_ref, table_ref, out_ref, w_ref, t_ref):
    step = pl.program_id(0)
    rows_in = t_ref.shape[0]
    coarse_count = rows_in - 4 * GHOST

    @pl.when(step == 0)
    def _():
        for t in range(NTYPE):
            w_ref[t * W : (t + 1) * W, :] = block_diagonal(table_ref[t], False)
        t_ref[:coarse_count, :] = ans_ref[...]
        for q, r in enumerate((r0, r1, r2, r3)):
            first = coarse_count + q * GHOST
            t_ref[first : first + GHOST, :] = r[...]

    target = columns(targets(dest_ref[...], slot_ref[...], coarse_count))
    fetched = jnp.dot(one_hot_columns(target, rows_in), t_ref[...], preferred_element_type=f32).astype(bf16)
    out_ref[...] = typed(fetched, columns(type_ref[...]), w_ref[...]).astype(bf16)


VMEM = pl.BlockSpec(memory_space=pltpu.VMEM)


def ghost_shape():
    return [jax.ShapeDtypeStruct((GHOST, W), bf16)] * 4


def whole(shape):
    return pl.BlockSpec(shape, lambda *_: (0,) * len(shape))


def restrict(x, meta, table, count):
    steps = x.shape[0] // CHUNK
    rows = count + 4 * GHOST
    meta_spec = pl.BlockSpec((CHUNK // LANES, LANES), lambda i: (i, 0))
    return pl.pallas_call(
        restrict_kernel,
        grid=(steps,),
        in_specs=[pl.BlockSpec((CHUNK, W), lambda i: (i, 0)), meta_spec, meta_spec, meta_spec, whole(table.shape)],
        out_specs=[VMEM] * 5,
        out_shape=[jax.ShapeDtypeStruct((count, W), f32)] + ghost_shape(),
        scratch_shapes=[pltpu.VMEM((NTYPE * W, W), bf16), pltpu.VMEM((rows, W), f32)],
        name="restrict",
    )(x, *meta, table)


def sweep(local, incoming, ghost, inverse):
    return pl.pallas_call(
        sweep_kernel,
        in_specs=[VMEM] * 7,
        out_specs=VMEM,
        out_shape=jax.ShapeDtypeStruct(local.shape, bf16),
        name="sweep",
    )(local, *incoming, ghost, inverse)


def couple(coef, first_sweep, halo, neighbours, coef_index, face_table, ghost, inverse):
    count = first_sweep.shape[0]
    return pl.pallas_call(
        couple_kernel,
        in_specs=[pl.BlockSpec(memory_space=pltpu.SMEM)] + [VMEM] * 10,
        out_specs=[VMEM] * 6,
        out_shape=[jax.ShapeDtypeStruct((count, W), f32), jax.ShapeDtypeStruct((count, W), bf16)] + ghost_shape(),
        scratch_shapes=[pltpu.VMEM((5 * count, W), bf16)],
        name="couple",
    )(coef, first_sweep, *halo, neighbours, coef_index, face_table, ghost, inverse)


def prolong(answer, returned, meta, table, fine_count):
    count = answer.shape[0]
    rows = count + 4 * GHOST
    meta_spec = pl.BlockSpec((CHUNK // LANES, LANES), lambda i: (i, 0))
    return pl.pallas_call(
        prolong_kernel,
        grid=(fine_count // CHUNK,),
        in_specs=[VMEM] * 5 + [meta_spec, meta_spec, meta_spec, whole(table.shape)],
        out_specs=pl.BlockSpec((CHUNK, W), lambda i: (i, 0)),
        out_shape=jax.ShapeDtypeStruct((fine_count, W), bf16),
        scratch_shapes=[pltpu.VMEM((NTYPE * W, W), bf16), pltpu.VMEM((rows, W), bf16)],
        name="prolong",
    )(answer, *returned, *meta, table)


def shards(
    fine_residual, dest_owner, coarse_slot, ghost_slot, child_type, restrict_table, inverse_blocks,
    face_table, face_coef, coef_index, neighbours,
):
    fine_count = fine_residual.shape[0]
    count = inverse_blocks.shape[0]
    perms = swap_pairs(lax.axis_size("px"), lax.axis_size("py"))
    meta = [m.reshape(fine_count // LANES, LANES) for m in (dest_owner, coarse_slot, child_type)]
    local, *outgoing = restrict(fine_residual, meta, restrict_table, count)
    incoming = exchange(outgoing, perms)
    first_sweep = sweep(local, incoming, ghost_slot, inverse_blocks)
    halo = exchange([first_sweep] * 4, perms)
    coarse_solution, answer, *replies = couple(
        face_coef, first_sweep, halo, neighbours, coef_index, face_table, ghost_slot, inverse_blocks
    )
    returned = exchange(replies, perms)
    fine_correction = prolong(answer, returned, meta, restrict_table, fine_count)
    return (coarse_solution, fine_correction)


def solution(mesh):
    both = ("px", "py")
    in_specs = (
        P(both, None), P(both), P(both), P(both, None), P(both), P(), P(both, None), P(), P(), P(None, both), P(None, both),
    )
    out_specs = (P(both, None), P(both, None))
    return jax.shard_map(shards, mesh=mesh, in_specs=in_specs, out_specs=out_specs, check_vma=False)
```

```python
import jax
import jax.numpy as jnp
from jax import lax
from jax.experimental import pallas as pl
from jax.experimental.pallas import tpu as pltpu
from jax.sharding import PartitionSpec as P


bf16 = jnp.bfloat16
f32 = jnp.float32
i32 = jnp.int32
i16 = jnp.int16

OMEGA = 0.5
DOF = 64
RHS = 4
W = 256
NTYPE = 8
FACES = 6
KINDS = 16
GHOST = 32
LANES = 128
CHUNK = 1024
RB = 128
PB = 512
VMEM_BYTES = 40 * 2**20


def swap_pairs(n_px, n_py):
    def at(a, b):
        return (a % n_px) * n_py + b % n_py

    perms = []
    for start in (0, 1):
        perm = []
        for b in range(n_py):
            for a in range(start, n_px + start, 2):
                perm += [(at(a, b), at(a + 1, b)), (at(a + 1, b), at(a, b))]
        perms.append(sorted(perm))
    for start in (0, 1):
        perm = []
        for a in range(n_px):
            for b in range(start, n_py + start, 2):
                perm += [(at(a, b), at(a, b + 1)), (at(a, b + 1), at(a, b))]
        perms.append(sorted(perm))
    return perms


def exchange(arrays, perms):
    moved = []
    for x, perm in zip(arrays, perms):
        moved.append(pltpu.with_memory_space_constraint(lax.ppermute(x, ("px", "py"), perm), pltpu.VMEM))
    return moved


def wide(column):
    return jnp.concatenate([column, column], axis=1)


def block_diagonal(matrix, flipped):
    row = lax.broadcasted_iota(i32, (W, DOF), 0) % DOF
    col = lax.broadcasted_iota(i32, (W, DOF), 1)
    spread = (row == col).astype(f32).astype(bf16)
    dims = (((1,), (1 if flipped else 0,)), ((), ()))
    half = lax.dot_general(spread, matrix, dims, preferred_element_type=f32).astype(bf16)
    full = lax.dot_general(half, spread, (((1,), (1,)), ((), ())), preferred_element_type=f32)
    r = lax.broadcasted_iota(i32, (W, W), 0) // DOF
    c = lax.broadcasted_iota(i32, (W, W), 1) // DOF
    return jnp.where(r == c, full, 0.0).astype(bf16)


def position():
    a, b = lax.axis_index("px"), lax.axis_index("py")
    n_py = lax.axis_size("py")
    return a * n_py + b, lax.rem(a, 2) == 0, lax.rem(b, 2) == 0


def partner(off, even_x, even_y):
    q_px = jnp.where((off > 0) == even_x, 0, 1)
    q_py = jnp.where((off > 0) == even_y, 2, 3)
    return jnp.where((off == 1) | (off == -1), q_py, q_px)


def targets(dest, slot, coarse_count):
    own, even_x, even_y = position()
    off = dest - own
    return jnp.where(off == 0, slot, coarse_count + partner(off, even_x, even_y) * GHOST + slot)


def list_rows(ghost):
    _, even_x, even_y = position()
    low_y, high_y, low_x, high_x = (ghost[j : j + 1, :] for j in range(4))
    ordered = [
        jnp.where(even_x, high_x, low_x),
        jnp.where(even_x, low_x, high_x),
        jnp.where(even_y, high_y, low_y),
        jnp.where(even_y, low_y, high_y),
    ]
    return jnp.broadcast_to(jnp.concatenate(ordered, axis=1), (8, 4 * GHOST))


def ones_where(mask):
    return jnp.where(mask, jnp.ones((), bf16), jnp.zeros((), bf16))


def one_hot_rows(values, row_count):
    row_id = lax.broadcasted_iota(i32, (row_count, LANES), 0).astype(i16)
    hits = []
    for r in range(values.shape[0]):
        wanted = jnp.broadcast_to(values[r : r + 1, :], (16, LANES)).astype(i16)
        wanted = jnp.concatenate([wanted] * (row_count // 16), axis=0)
        hits.append(ones_where(row_id == wanted))
    return jnp.concatenate(hits, axis=1)


def columns(rows):
    flipped = rows.T
    parts = [
        jnp.broadcast_to(flipped[:, r : r + 1], (LANES, LANES)).astype(i16) for r in range(rows.shape[0])
    ]
    return jnp.concatenate(parts, axis=0)


def one_hot_columns(column, row_count):
    lane = lax.broadcasted_iota(i32, column.shape, 1).astype(i16)
    return jnp.concatenate(
        [ones_where(column - jnp.asarray(k * LANES, i16) == lane) for k in range(row_count // LANES)], axis=1
    )


def typed(x_rows, kinds, table, rows):
    outs = []
    for r in range(0, x_rows.shape[0], rows):
        x, kind = x_rows[r : r + rows], kinds[r : r + rows]
        parts = [x * wide(ones_where(kind == jnp.asarray(t, i16))) for t in range(NTYPE)]
        outs.append(jnp.dot(jnp.concatenate(parts, axis=1), table, preferred_element_type=f32).astype(bf16))
    return jnp.concatenate(outs, axis=0)


def restrict_kernel(
    x_ref, dest_ref, slot_ref, type_ref, table_ref, inv_hbm, local_ref, g0, g1, g2, g3, inv_ref, w_ref, acc_ref, sem
):
    step = pl.program_id(0)
    rows_out = acc_ref.shape[0]
    coarse_count = rows_out - 4 * GHOST

    load = pltpu.make_async_copy(inv_hbm, inv_ref, sem)

    @pl.when(step == 0)
    def _():
        load.start()
        for t in range(NTYPE):
            w_ref[t * W : (t + 1) * W, :] = block_diagonal(table_ref[t], True)
        acc_ref[...] = jnp.zeros_like(acc_ref)

    contrib = typed(x_ref[...], columns(type_ref[...]), w_ref[...], RB)
    hits = one_hot_rows(targets(dest_ref[...], slot_ref[...], coarse_count), rows_out)
    acc_ref[...] += jnp.dot(hits, contrib, preferred_element_type=f32)

    @pl.when(step == pl.num_programs(0) - 1)
    def _():
        local_ref[...] = acc_ref[:coarse_count, :]
        for q, out in enumerate((g0, g1, g2, g3)):
            first = coarse_count + q * GHOST
            out[...] = acc_ref[first : first + GHOST, :].astype(bf16)
        load.wait()


def apply_blocks(inv_ref, v):
    count = v.shape[0]
    lane = lax.broadcasted_iota(i32, (count, LANES), 1)
    row = lax.broadcasted_iota(i32, (DOF * DOF, DOF), 0)
    col = lax.broadcasted_iota(i32, (DOF * DOF, DOF), 1)
    summing = (col == row // DOF).astype(f32).astype(bf16)
    outs = []
    for s in range(RHS):
        tile = v[:, (s // 2) * LANES : (s // 2 + 1) * LANES].astype(f32)
        turned = pltpu.roll(tile, DOF, 1)
        low, high = (tile, turned) if s % 2 == 0 else (turned, tile)
        doubled = jnp.where(lane < DOF, low, high).astype(bf16)
        products = jnp.concatenate(
            [inv_ref[:, k * LANES : (k + 1) * LANES] * doubled for k in range(DOF * DOF // LANES)], axis=1
        )
        outs.append(jnp.dot(products, summing, preferred_element_type=f32))
    return jnp.concatenate(outs, axis=1)


def sweep_kernel(local_ref, i0, i1, i2, i3, ghost_ref, inv_ref, out_ref):
    count = local_ref.shape[0]
    hits = one_hot_rows(list_rows(ghost_ref[...])[:1], count)
    incoming = jnp.concatenate([i0[...], i1[...], i2[...], i3[...]], axis=0)
    rhs = local_ref[...] + jnp.dot(hits, incoming, preferred_element_type=f32)
    out_ref[...] = apply_blocks(inv_ref, rhs.astype(bf16)).astype(bf16)


def couple_kernel(
    coef_ref, fs_ref, h0, h1, h2, h3, nb_ref, ci_ref, face_ref, ghost_ref, inv_ref,
    sol_ref, ans_ref, r0, r1, r2, r3,
):
    count = fs_ref.shape[0]
    own, even_x, even_y = position()
    nb = nb_ref[...]
    off = nb // count - own
    block = jnp.where(off == 0, 0, 1 + partner(off, even_x, even_y))
    index_t = (nb % count).T
    block_t = block.T
    scale = jnp.zeros(nb.shape, f32)
    for k in range(KINDS):
        scale = jnp.where(ci_ref[...] == k, coef_ref[k], scale)
    scale_t = scale.T
    coupled = jnp.zeros((count, W), f32)
    for f in range(FACES):
        column = jnp.broadcast_to(index_t[:, f : f + 1], (count, LANES)).astype(i16)
        hits = one_hot_columns(column, count)
        where = wide(jnp.broadcast_to(block_t[:, f : f + 1], (count, LANES)))
        beside = jnp.dot(hits, fs_ref[...], preferred_element_type=f32)
        for q, source in enumerate((h0, h1, h2, h3)):
            beside = jnp.where(where == q + 1, jnp.dot(hits, source[...], preferred_element_type=f32), beside)
        term = jnp.dot(beside.astype(bf16), block_diagonal(face_ref[f], True), preferred_element_type=f32)
        coupled = coupled + term * wide(jnp.broadcast_to(scale_t[:, f : f + 1], (count, LANES)))
    correction = apply_blocks(inv_ref, coupled.astype(bf16))
    solution_rows = fs_ref[...].astype(f32) - OMEGA * correction
    sol_ref[...] = solution_rows
    answer = solution_rows.astype(bf16)
    ans_ref[...] = answer
    listed = jnp.broadcast_to(list_rows(ghost_ref[...]).T[:, :1], (4 * GHOST, LANES)).astype(i16)
    replies = jnp.dot(one_hot_columns(listed, count), answer, preferred_element_type=f32).astype(bf16)
    for q, out in enumerate((r0, r1, r2, r3)):
        out[...] = replies[q * GHOST : (q + 1) * GHOST, :]


def prolong_kernel(ans_ref, r0, r1, r2, r3, dest_ref, slot_ref, type_ref, table_ref, out_ref, w_ref, t_ref):
    step = pl.program_id(0)
    rows_in = t_ref.shape[0]
    coarse_count = rows_in - 4 * GHOST

    @pl.when(step == 0)
    def _():
        for t in range(NTYPE):
            w_ref[t * W : (t + 1) * W, :] = block_diagonal(table_ref[t], False)
        t_ref[:coarse_count, :] = ans_ref[...]
        for q, r in enumerate((r0, r1, r2, r3)):
            first = coarse_count + q * GHOST
            t_ref[first : first + GHOST, :] = r[...]

    target = columns(targets(dest_ref[...], slot_ref[...], coarse_count))
    fetched = jnp.dot(one_hot_columns(target, rows_in), t_ref[...], preferred_element_type=f32).astype(bf16)
    out_ref[...] = typed(fetched, columns(type_ref[...]), w_ref[...], PB)


VMEM = pl.BlockSpec(memory_space=pltpu.VMEM)


def in_hbm(x):
    return pltpu.with_memory_space_constraint(x, pltpu.HBM)


def ghost_shape():
    return [pltpu.VMEM((GHOST, W), bf16)] * 4


def whole(shape):
    return pl.BlockSpec(shape, lambda *_: (0,) * len(shape))


def restrict(x, meta, table, inverse):
    count = inverse.shape[0]
    steps = x.shape[0] // CHUNK
    rows = count + 4 * GHOST
    meta_spec = pl.BlockSpec((CHUNK // LANES, LANES), lambda i: (i, 0))
    return pl.pallas_call(
        restrict_kernel,
        grid=(steps,),
        in_specs=[pl.BlockSpec((CHUNK, W), lambda i: (i, 0)), meta_spec, meta_spec, meta_spec, whole(table.shape), pl.BlockSpec(memory_space=pltpu.HBM)],
        out_specs=[VMEM] * 6,
        out_shape=[pltpu.VMEM((count, W), f32)] + ghost_shape() + [pltpu.VMEM(inverse.shape, bf16)],
        scratch_shapes=[pltpu.VMEM((NTYPE * W, W), bf16), pltpu.VMEM((rows, W), f32), pltpu.SemaphoreType.DMA],
        compiler_params=pltpu.CompilerParams(vmem_limit_bytes=VMEM_BYTES),
        name="restrict",
    )(x, *meta, table, inverse)


def sweep(local, incoming, ghost, inverse):
    return pl.pallas_call(
        sweep_kernel,
        in_specs=[VMEM] * 7,
        out_specs=VMEM,
        out_shape=pltpu.VMEM(local.shape, bf16),
        compiler_params=pltpu.CompilerParams(vmem_limit_bytes=VMEM_BYTES),
        name="sweep",
    )(local, *incoming, ghost, inverse)


def couple(coef, first_sweep, halo, neighbours, coef_index, face_table, ghost, inverse):
    count = first_sweep.shape[0]
    return pl.pallas_call(
        couple_kernel,
        in_specs=[pl.BlockSpec(memory_space=pltpu.SMEM)] + [VMEM] * 10,
        out_specs=[VMEM] * 6,
        out_shape=[jax.ShapeDtypeStruct((count, W), f32), pltpu.VMEM((count, W), bf16)] + ghost_shape(),
        compiler_params=pltpu.CompilerParams(vmem_limit_bytes=VMEM_BYTES),
        name="couple",
    )(coef, first_sweep, *halo, neighbours, coef_index, face_table, ghost, inverse)


def prolong(answer, returned, meta, table, fine_count):
    count = answer.shape[0]
    rows = count + 4 * GHOST
    meta_spec = pl.BlockSpec((CHUNK // LANES, LANES), lambda i: (i, 0))
    return pl.pallas_call(
        prolong_kernel,
        grid=(fine_count // CHUNK,),
        in_specs=[VMEM] * 5 + [meta_spec, meta_spec, meta_spec, whole(table.shape)],
        out_specs=pl.BlockSpec((CHUNK, W), lambda i: (i, 0)),
        out_shape=jax.ShapeDtypeStruct((fine_count, W), bf16),
        scratch_shapes=[pltpu.VMEM((NTYPE * W, W), bf16), pltpu.VMEM((rows, W), bf16)],
        compiler_params=pltpu.CompilerParams(vmem_limit_bytes=VMEM_BYTES),
        name="prolong",
    )(answer, *returned, *meta, table)


def shards(
    fine_residual, dest_owner, coarse_slot, ghost_slot, child_type, restrict_table, inverse_blocks,
    face_table, face_coef, coef_index, neighbours,
):
    fine_count = fine_residual.shape[0]
    perms = swap_pairs(lax.axis_size("px"), lax.axis_size("py"))
    meta = [m.reshape(fine_count // LANES, LANES) for m in (dest_owner, coarse_slot, child_type)]
    local, *outgoing, inverse = restrict(
        in_hbm(fine_residual), [in_hbm(m) for m in meta], in_hbm(restrict_table), in_hbm(inverse_blocks)
    )
    incoming = exchange(outgoing, perms)
    first_sweep = sweep(local, incoming, ghost_slot, inverse)
    halo = exchange([first_sweep] * 4, perms)
    coarse_solution, answer, *replies = couple(
        face_coef, first_sweep, halo, neighbours, coef_index, face_table, ghost_slot, inverse
    )
    returned = exchange(replies, perms)
    fine_correction = prolong(answer, returned, meta, restrict_table, fine_count)
    return (coarse_solution, fine_correction)


def solution(mesh):
    both = ("px", "py")
    in_specs = (
        P(both, None), P(both), P(both), P(both, None), P(both), P(), P(both, None), P(), P(), P(None, both), P(None, both),
    )
    out_specs = (P(both, None), P(both, None))
    return jax.shard_map(shards, mesh=mesh, in_specs=in_specs, out_specs=out_specs, check_vma=False)
```

```python
import functools

import jax
import jax.numpy as jnp
from jax import lax
from jax.experimental import pallas as pl
from jax.experimental.pallas import tpu as pltpu
from jax.sharding import PartitionSpec as P


bf16 = jnp.bfloat16
f32 = jnp.float32
i32 = jnp.int32
i16 = jnp.int16

OMEGA = 0.5
DOF = 64
RHS = 4
W = 256
NTYPE = 8
FACES = 6
KINDS = 16
GHOST = 32
LANES = 128
CHUNK = 1024
RB = 128
PB = 512
VMEM_BYTES = 40 * 2**20


def swap_pairs(n_px, n_py):
    def at(a, b):
        return (a % n_px) * n_py + b % n_py

    perms = []
    for start in (0, 1):
        perm = []
        for b in range(n_py):
            for a in range(start, n_px + start, 2):
                perm += [(at(a, b), at(a + 1, b)), (at(a + 1, b), at(a, b))]
        perms.append(sorted(perm))
    for start in (0, 1):
        perm = []
        for a in range(n_px):
            for b in range(start, n_py + start, 2):
                perm += [(at(a, b), at(a, b + 1)), (at(a, b + 1), at(a, b))]
        perms.append(sorted(perm))
    return perms


def exchange(arrays, perms):
    moved = []
    for x, perm in zip(arrays, perms):
        moved.append(pltpu.with_memory_space_constraint(lax.ppermute(x, ("px", "py"), perm), pltpu.VMEM))
    return moved


def wide(column):
    return jnp.concatenate([column, column], axis=1)


def block_diagonal(matrix, flipped):
    row = lax.broadcasted_iota(i32, (W, DOF), 0) % DOF
    col = lax.broadcasted_iota(i32, (W, DOF), 1)
    spread = (row == col).astype(f32).astype(bf16)
    dims = (((1,), (1 if flipped else 0,)), ((), ()))
    half = lax.dot_general(spread, matrix, dims, preferred_element_type=f32).astype(bf16)
    full = lax.dot_general(half, spread, (((1,), (1,)), ((), ())), preferred_element_type=f32)
    r = lax.broadcasted_iota(i32, (W, W), 0) // DOF
    c = lax.broadcasted_iota(i32, (W, W), 1) // DOF
    return jnp.where(r == c, full, 0.0).astype(bf16)


def position():
    a, b = lax.axis_index("px"), lax.axis_index("py")
    n_py = lax.axis_size("py")
    return a * n_py + b, lax.rem(a, 2) == 0, lax.rem(b, 2) == 0


def partner(off, even_x, even_y):
    q_px = jnp.where((off > 0) == even_x, 0, 1)
    q_py = jnp.where((off > 0) == even_y, 2, 3)
    return jnp.where((off == 1) | (off == -1), q_py, q_px)


def targets(dest, slot, coarse_count):
    own, even_x, even_y = position()
    off = dest - own
    return jnp.where(off == 0, slot, coarse_count + partner(off, even_x, even_y) * GHOST + slot)


def list_rows(ghost):
    _, even_x, even_y = position()
    low_y, high_y, low_x, high_x = (ghost[j : j + 1, :] for j in range(4))
    ordered = [
        jnp.where(even_x, high_x, low_x),
        jnp.where(even_x, low_x, high_x),
        jnp.where(even_y, high_y, low_y),
        jnp.where(even_y, low_y, high_y),
    ]
    return jnp.broadcast_to(jnp.concatenate(ordered, axis=1), (8, 4 * GHOST))


def ones_where(mask):
    return jnp.where(mask, jnp.ones((), bf16), jnp.zeros((), bf16))


def one_hot_rows(values, row_count):
    row_id = lax.broadcasted_iota(i32, (row_count, LANES), 0).astype(i16)
    hits = []
    for r in range(values.shape[0]):
        wanted = jnp.broadcast_to(values[r : r + 1, :], (16, LANES)).astype(i16)
        wanted = jnp.concatenate([wanted] * (row_count // 16), axis=0)
        hits.append(ones_where(row_id == wanted))
    return jnp.concatenate(hits, axis=1)


def columns(rows):
    flipped = rows.T
    parts = [
        jnp.broadcast_to(flipped[:, r : r + 1], (LANES, LANES)).astype(i16) for r in range(rows.shape[0])
    ]
    return jnp.concatenate(parts, axis=0)


def one_hot_columns(column, row_count):
    lane = lax.broadcasted_iota(i32, column.shape, 1).astype(i16)
    return jnp.concatenate(
        [ones_where(column - jnp.asarray(k * LANES, i16) == lane) for k in range(row_count // LANES)], axis=1
    )


def typed(x_rows, kinds, table, rows):
    outs = []
    for r in range(0, x_rows.shape[0], rows):
        x, kind = x_rows[r : r + rows], kinds[r : r + rows]
        parts = [x * wide(ones_where(kind == jnp.asarray(t, i16))) for t in range(NTYPE)]
        outs.append(jnp.dot(jnp.concatenate(parts, axis=1), table, preferred_element_type=f32).astype(bf16))
    return jnp.concatenate(outs, axis=0)


def restrict_kernel(
    x_ref, dest_ref, slot_ref, type_ref, table_ref, inv_hbm, local_ref, g0, g1, g2, g3, inv_ref, w_ref, acc_ref, sem
):
    step = pl.program_id(0)
    rows_out = acc_ref.shape[0]
    coarse_count = rows_out - 4 * GHOST

    load = pltpu.make_async_copy(inv_hbm, inv_ref, sem)

    @pl.when(step == 0)
    def _():
        load.start()
        for t in range(NTYPE):
            w_ref[t * W : (t + 1) * W, :] = block_diagonal(table_ref[t], True)
        acc_ref[...] = jnp.zeros_like(acc_ref)

    contrib = typed(x_ref[...], columns(type_ref[...]), w_ref[...], RB)
    hits = one_hot_rows(targets(dest_ref[...], slot_ref[...], coarse_count), rows_out)
    acc_ref[...] += jnp.dot(hits, contrib, preferred_element_type=f32)

    @pl.when(step == pl.num_programs(0) - 1)
    def _():
        local_ref[...] = acc_ref[:coarse_count, :]
        for q, out in enumerate((g0, g1, g2, g3)):
            first = coarse_count + q * GHOST
            out[...] = acc_ref[first : first + GHOST, :].astype(bf16)
        load.wait()


def apply_blocks(inv_ref, v):
    count = v.shape[0]
    lane = lax.broadcasted_iota(i32, (count, LANES), 1)
    row = lax.broadcasted_iota(i32, (DOF * DOF, DOF), 0)
    col = lax.broadcasted_iota(i32, (DOF * DOF, DOF), 1)
    summing = (col == row // DOF).astype(f32).astype(bf16)
    outs = []
    for s in range(RHS):
        tile = v[:, (s // 2) * LANES : (s // 2 + 1) * LANES].astype(f32)
        turned = pltpu.roll(tile, DOF, 1)
        low, high = (tile, turned) if s % 2 == 0 else (turned, tile)
        doubled = jnp.where(lane < DOF, low, high).astype(bf16)
        products = jnp.concatenate(
            [inv_ref[:, k * LANES : (k + 1) * LANES] * doubled for k in range(DOF * DOF // LANES)], axis=1
        )
        outs.append(jnp.dot(products, summing, preferred_element_type=f32))
    return jnp.concatenate(outs, axis=1)


def sweep_kernel(local_ref, i0, i1, i2, i3, ghost_ref, inv_ref, out_ref):
    count = local_ref.shape[0]
    hits = one_hot_rows(list_rows(ghost_ref[...])[:1], count)
    incoming = jnp.concatenate([i0[...], i1[...], i2[...], i3[...]], axis=0)
    rhs = local_ref[...] + jnp.dot(hits, incoming, preferred_element_type=f32)
    out_ref[...] = apply_blocks(inv_ref, rhs.astype(bf16)).astype(bf16)


def own_rows_kernel(fs_ref, nb_ref, face_ref, hits_ref, own_ref, faces_ref):
    count = fs_ref.shape[0]
    index_t = (nb_ref[...] % count).T
    for f in range(FACES):
        column = jnp.broadcast_to(index_t[:, f : f + 1], (count, LANES)).astype(i16)
        hits = one_hot_columns(column, count)
        rows = slice(f * count, (f + 1) * count)
        hits_ref[rows, :] = hits
        own_ref[rows, :] = jnp.dot(hits, fs_ref[...], preferred_element_type=f32).astype(bf16)
        faces_ref[f * W : (f + 1) * W, :] = block_diagonal(face_ref[f], True)


def couple_kernel(
    coef_ref, fs_ref, h0, h1, h2, h3, nb_ref, ci_ref, hits_ref, own_ref, faces_ref, ghost_ref, inv_ref,
    sol_ref, ans_ref, r0, r1, r2, r3,
):
    count = fs_ref.shape[0]
    own, even_x, even_y = position()
    off = nb_ref[...] // count - own
    block_t = jnp.where(off == 0, 0, 1 + partner(off, even_x, even_y)).T
    scale = jnp.zeros(off.shape, f32)
    for k in range(KINDS):
        scale = jnp.where(ci_ref[...] == k, coef_ref[k], scale)
    scale_t = scale.T
    coupled = jnp.zeros((count, W), f32)
    for f in range(FACES):
        rows = slice(f * count, (f + 1) * count)
        where = wide(jnp.broadcast_to(block_t[:, f : f + 1], (count, LANES)).astype(i16))
        beside = own_ref[rows, :]
        for q, source in enumerate((h0, h1, h2, h3)):
            found = jnp.dot(hits_ref[rows, :], source[...], preferred_element_type=f32).astype(bf16)
            beside = jnp.where(where == jnp.asarray(q + 1, i16), found, beside)
        term = jnp.dot(beside, faces_ref[f * W : (f + 1) * W, :], preferred_element_type=f32)
        coupled = coupled + term * wide(jnp.broadcast_to(scale_t[:, f : f + 1], (count, LANES)))
    correction = apply_blocks(inv_ref, coupled.astype(bf16))
    solution_rows = fs_ref[...].astype(f32) - OMEGA * correction
    sol_ref[...] = solution_rows
    answer = solution_rows.astype(bf16)
    ans_ref[...] = answer
    listed = jnp.broadcast_to(list_rows(ghost_ref[...]).T[:, :1], (4 * GHOST, LANES)).astype(i16)
    replies = jnp.dot(one_hot_columns(listed, count), answer, preferred_element_type=f32).astype(bf16)
    for q, out in enumerate((r0, r1, r2, r3)):
        out[...] = replies[q * GHOST : (q + 1) * GHOST, :]


def fetch_kernel(ans_ref, dest_ref, slot_ref, table_ref, out_ref, w_ref):
    count = ans_ref.shape[0]
    for t in range(NTYPE):
        w_ref[t * W : (t + 1) * W, :] = block_diagonal(table_ref[t], False)
    target = targets(dest_ref[...], slot_ref[...], count)
    for g in range(out_ref.shape[0] // CHUNK):
        column = columns(target[g * (CHUNK // LANES) : (g + 1) * (CHUNK // LANES), :])
        for r in range(0, CHUNK, PB):
            hits = one_hot_columns(column[r : r + PB, :], count)
            first = g * CHUNK + r
            out_ref[first : first + PB, :] = jnp.dot(hits, ans_ref[...], preferred_element_type=f32).astype(bf16)


def prolong_kernel(count, local_ref, r0, r1, r2, r3, w_ref, dest_ref, slot_ref, type_ref, out_ref):
    step = pl.program_id(0)
    target = columns(targets(dest_ref[...], slot_ref[...], count) - count)
    returned = jnp.concatenate([r0[...], r1[...], r2[...], r3[...]], axis=0)
    remote = jnp.dot(one_hot_columns(target, 4 * GHOST), returned, preferred_element_type=f32)
    local = local_ref[pl.ds(pl.multiple_of(step * CHUNK, CHUNK), CHUNK), :]
    fetched = (local.astype(f32) + remote).astype(bf16)
    out_ref[...] = typed(fetched, columns(type_ref[...]), w_ref[...], PB)


VMEM = pl.BlockSpec(memory_space=pltpu.VMEM)


def in_hbm(x):
    return pltpu.with_memory_space_constraint(x, pltpu.HBM)


def ghost_shape():
    return [pltpu.VMEM((GHOST, W), bf16)] * 4


def whole(shape):
    return pl.BlockSpec(shape, lambda *_: (0,) * len(shape))


def restrict(x, meta, table, inverse):
    count = inverse.shape[0]
    steps = x.shape[0] // CHUNK
    rows = count + 4 * GHOST
    meta_spec = pl.BlockSpec((CHUNK // LANES, LANES), lambda i: (i, 0))
    return pl.pallas_call(
        restrict_kernel,
        grid=(steps,),
        in_specs=[pl.BlockSpec((CHUNK, W), lambda i: (i, 0)), meta_spec, meta_spec, meta_spec, whole(table.shape), pl.BlockSpec(memory_space=pltpu.HBM)],
        out_specs=[VMEM] * 6,
        out_shape=[pltpu.VMEM((count, W), f32)] + ghost_shape() + [pltpu.VMEM(inverse.shape, bf16)],
        scratch_shapes=[pltpu.VMEM((NTYPE * W, W), bf16), pltpu.VMEM((rows, W), f32), pltpu.SemaphoreType.DMA],
        compiler_params=pltpu.CompilerParams(vmem_limit_bytes=VMEM_BYTES),
        name="restrict",
    )(x, *meta, table, inverse)


def sweep(local, incoming, ghost, inverse):
    return pl.pallas_call(
        sweep_kernel,
        in_specs=[VMEM] * 7,
        out_specs=VMEM,
        out_shape=pltpu.VMEM(local.shape, bf16),
        compiler_params=pltpu.CompilerParams(vmem_limit_bytes=VMEM_BYTES),
        name="sweep",
    )(local, *incoming, ghost, inverse)


def own_rows(first_sweep, neighbours, face_table):
    count = first_sweep.shape[0]
    return pl.pallas_call(
        own_rows_kernel,
        in_specs=[VMEM] * 3,
        out_specs=[VMEM] * 3,
        out_shape=[
            pltpu.VMEM((FACES * count, count), bf16), pltpu.VMEM((FACES * count, W), bf16), pltpu.VMEM((FACES * W, W), bf16)
        ],
        compiler_params=pltpu.CompilerParams(vmem_limit_bytes=VMEM_BYTES),
        name="own_rows",
    )(first_sweep, neighbours, face_table)


def couple(coef, first_sweep, halo, neighbours, coef_index, prepared, ghost, inverse):
    count = first_sweep.shape[0]
    return pl.pallas_call(
        couple_kernel,
        in_specs=[pl.BlockSpec(memory_space=pltpu.SMEM)] + [VMEM] * 12,
        out_specs=[VMEM] * 6,
        out_shape=[jax.ShapeDtypeStruct((count, W), f32), pltpu.VMEM((count, W), bf16)] + ghost_shape(),
        compiler_params=pltpu.CompilerParams(vmem_limit_bytes=VMEM_BYTES),
        name="couple",
    )(coef, first_sweep, *halo, neighbours, coef_index, *prepared, ghost, inverse)


def fetch(answer, meta, table):
    fine_count = meta[0].shape[0] * LANES
    return pl.pallas_call(
        fetch_kernel,
        in_specs=[VMEM] * 4,
        out_specs=[VMEM] * 2,
        out_shape=[pltpu.VMEM((fine_count, W), bf16), pltpu.VMEM((NTYPE * W, W), bf16)],
        compiler_params=pltpu.CompilerParams(vmem_limit_bytes=VMEM_BYTES),
        name="fetch",
    )(answer, meta[0], meta[1], table)


def prolong(local, returned, table, meta, count):
    fine_count = local.shape[0]
    meta_spec = pl.BlockSpec((CHUNK // LANES, LANES), lambda i: (i, 0))
    return pl.pallas_call(
        functools.partial(prolong_kernel, count),
        grid=(fine_count // CHUNK,),
        in_specs=[VMEM] * 6 + [meta_spec, meta_spec, meta_spec],
        out_specs=pl.BlockSpec((CHUNK, W), lambda i: (i, 0)),
        out_shape=jax.ShapeDtypeStruct((fine_count, W), bf16),
        compiler_params=pltpu.CompilerParams(vmem_limit_bytes=VMEM_BYTES),
        name="prolong",
    )(local, *returned, table, *meta)


def shards(
    fine_residual, dest_owner, coarse_slot, ghost_slot, child_type, restrict_table, inverse_blocks,
    face_table, face_coef, coef_index, neighbours,
):
    fine_count = fine_residual.shape[0]
    perms = swap_pairs(lax.axis_size("px"), lax.axis_size("py"))
    meta = [m.reshape(fine_count // LANES, LANES) for m in (dest_owner, coarse_slot, child_type)]
    local, *outgoing, inverse = restrict(
        in_hbm(fine_residual), [in_hbm(m) for m in meta], in_hbm(restrict_table), in_hbm(inverse_blocks)
    )
    incoming = exchange(outgoing, perms)
    first_sweep = sweep(local, incoming, ghost_slot, inverse)
    halo = exchange([first_sweep] * 4, perms)
    prepared = own_rows(first_sweep, neighbours, face_table)
    coarse_solution, answer, *replies = couple(
        face_coef, first_sweep, halo, neighbours, coef_index, prepared, ghost_slot, inverse
    )
    returned = exchange(replies, perms)
    fetched, table = fetch(answer, meta, restrict_table)
    fine_correction = prolong(fetched, returned, table, meta, inverse_blocks.shape[0])
    return (coarse_solution, fine_correction)


def solution(mesh):
    both = ("px", "py")
    in_specs = (
        P(both, None), P(both), P(both), P(both, None), P(both), P(), P(both, None), P(), P(), P(None, both), P(None, both),
    )
    out_specs = (P(both, None), P(both, None))
    return jax.shard_map(shards, mesh=mesh, in_specs=in_specs, out_specs=out_specs, check_vma=False)
```

```python
import functools

import jax
import jax.numpy as jnp
from jax import lax
from jax.experimental import pallas as pl
from jax.experimental.pallas import tpu as pltpu
from jax.sharding import PartitionSpec as P


bf16 = jnp.bfloat16
f32 = jnp.float32
i32 = jnp.int32
i16 = jnp.int16

OMEGA = 0.5
DOF = 64
RHS = 4
W = 256
NTYPE = 8
FACES = 6
KINDS = 16
GHOST = 32
LANES = 128
CHUNK = 1024
RB = 128
PB = 512
VMEM_BYTES = 40 * 2**20


def swap_pairs(n_px, n_py):
    def at(a, b):
        return (a % n_px) * n_py + b % n_py

    perms = []
    for start in (0, 1):
        perm = []
        for b in range(n_py):
            for a in range(start, n_px + start, 2):
                perm += [(at(a, b), at(a + 1, b)), (at(a + 1, b), at(a, b))]
        perms.append(sorted(perm))
    for start in (0, 1):
        perm = []
        for a in range(n_px):
            for b in range(start, n_py + start, 2):
                perm += [(at(a, b), at(a, b + 1)), (at(a, b + 1), at(a, b))]
        perms.append(sorted(perm))
    return perms


def exchange(arrays, perms):
    moved = []
    for x, perm in zip(arrays, perms):
        moved.append(pltpu.with_memory_space_constraint(lax.ppermute(x, ("px", "py"), perm), pltpu.VMEM))
    return moved


def wide(column):
    return jnp.concatenate([column, column], axis=1)


def block_diagonal(matrix, flipped):
    row = lax.broadcasted_iota(i32, (W, DOF), 0) % DOF
    col = lax.broadcasted_iota(i32, (W, DOF), 1)
    spread = (row == col).astype(f32).astype(bf16)
    dims = (((1,), (1 if flipped else 0,)), ((), ()))
    half = lax.dot_general(spread, matrix, dims, preferred_element_type=f32).astype(bf16)
    full = lax.dot_general(half, spread, (((1,), (1,)), ((), ())), preferred_element_type=f32)
    r = lax.broadcasted_iota(i32, (W, W), 0) // DOF
    c = lax.broadcasted_iota(i32, (W, W), 1) // DOF
    return jnp.where(r == c, full, 0.0).astype(bf16)


def position():
    a, b = lax.axis_index("px"), lax.axis_index("py")
    n_py = lax.axis_size("py")
    return a * n_py + b, lax.rem(a, 2) == 0, lax.rem(b, 2) == 0


def partner(off, even_x, even_y):
    q_px = jnp.where((off > 0) == even_x, 0, 1)
    q_py = jnp.where((off > 0) == even_y, 2, 3)
    return jnp.where((off == 1) | (off == -1), q_py, q_px)


def targets(dest, slot, coarse_count):
    own, even_x, even_y = position()
    off = dest - own
    return jnp.where(off == 0, slot, coarse_count + partner(off, even_x, even_y) * GHOST + slot)


def list_rows(ghost):
    _, even_x, even_y = position()
    low_y, high_y, low_x, high_x = (ghost[j : j + 1, :] for j in range(4))
    ordered = [
        jnp.where(even_x, high_x, low_x),
        jnp.where(even_x, low_x, high_x),
        jnp.where(even_y, high_y, low_y),
        jnp.where(even_y, low_y, high_y),
    ]
    return jnp.broadcast_to(jnp.concatenate(ordered, axis=1), (8, 4 * GHOST))


def ones_where(mask):
    return jnp.where(mask, jnp.ones((), bf16), jnp.zeros((), bf16))


def one_hot_rows(values, row_count):
    row_id = lax.broadcasted_iota(i32, (row_count, LANES), 0).astype(i16)
    hits = []
    for r in range(values.shape[0]):
        wanted = jnp.broadcast_to(values[r : r + 1, :], (16, LANES)).astype(i16)
        wanted = jnp.concatenate([wanted] * (row_count // 16), axis=0)
        hits.append(ones_where(row_id == wanted))
    return jnp.concatenate(hits, axis=1)


def columns(rows):
    flipped = rows.T
    parts = [
        jnp.broadcast_to(flipped[:, r : r + 1], (LANES, LANES)).astype(i16) for r in range(rows.shape[0])
    ]
    return jnp.concatenate(parts, axis=0)


def one_hot_columns(column, row_count):
    lane = lax.broadcasted_iota(i32, column.shape, 1).astype(i16)
    return jnp.concatenate(
        [ones_where(column - jnp.asarray(k * LANES, i16) == lane) for k in range(row_count // LANES)], axis=1
    )


def typed(x_rows, kinds, table, rows):
    outs = []
    for r in range(0, x_rows.shape[0], rows):
        x, kind = x_rows[r : r + rows], kinds[r : r + rows]
        parts = [x * wide(ones_where(kind == jnp.asarray(t, i16))) for t in range(NTYPE)]
        outs.append(jnp.dot(jnp.concatenate(parts, axis=1), table, preferred_element_type=f32).astype(bf16))
    return jnp.concatenate(outs, axis=0)


def restrict_kernel(
    x_ref, dest_ref, slot_ref, type_ref, table_ref, inv_hbm, contrib_ref, g0, g1, g2, g3, inv_ref, w_ref, acc_ref, sem
):
    step = pl.program_id(0)
    coarse_count = inv_ref.shape[0]

    load = pltpu.make_async_copy(inv_hbm, inv_ref, sem)

    @pl.when(step == 0)
    def _():
        load.start()
        for t in range(NTYPE):
            w_ref[t * W : (t + 1) * W, :] = block_diagonal(table_ref[t], True)
        acc_ref[...] = jnp.zeros_like(acc_ref)

    contrib = typed(x_ref[...], columns(type_ref[...]), w_ref[...], RB)
    contrib_ref[pl.ds(pl.multiple_of(step * CHUNK, CHUNK), CHUNK), :] = contrib
    remote = targets(dest_ref[...], slot_ref[...], coarse_count) - coarse_count
    acc_ref[...] += jnp.dot(one_hot_rows(remote, 4 * GHOST), contrib, preferred_element_type=f32)

    @pl.when(step == pl.num_programs(0) - 1)
    def _():
        for q, out in enumerate((g0, g1, g2, g3)):
            out[...] = acc_ref[q * GHOST : (q + 1) * GHOST, :].astype(bf16)
        load.wait()


def local_kernel(contrib_ref, dest_ref, slot_ref, out_ref):
    count = out_ref.shape[0]
    target = targets(dest_ref[...], slot_ref[...], count)
    group = CHUNK // LANES
    total = jnp.zeros(out_ref.shape, f32)
    for g in range(contrib_ref.shape[0] // CHUNK):
        hits = one_hot_rows(target[g * group : (g + 1) * group, :], count)
        total = total + jnp.dot(hits, contrib_ref[g * CHUNK : (g + 1) * CHUNK, :], preferred_element_type=f32)
    out_ref[...] = total


def apply_blocks(inv_ref, v):
    count = v.shape[0]
    lane = lax.broadcasted_iota(i32, (count, LANES), 1)
    row = lax.broadcasted_iota(i32, (DOF * DOF, DOF), 0)
    col = lax.broadcasted_iota(i32, (DOF * DOF, DOF), 1)
    summing = (col == row // DOF).astype(f32).astype(bf16)
    outs = []
    for s in range(RHS):
        tile = v[:, (s // 2) * LANES : (s // 2 + 1) * LANES].astype(f32)
        turned = pltpu.roll(tile, DOF, 1)
        low, high = (tile, turned) if s % 2 == 0 else (turned, tile)
        doubled = jnp.where(lane < DOF, low, high).astype(bf16)
        products = jnp.concatenate(
            [inv_ref[:, k * LANES : (k + 1) * LANES] * doubled for k in range(DOF * DOF // LANES)], axis=1
        )
        outs.append(jnp.dot(products, summing, preferred_element_type=f32))
    return jnp.concatenate(outs, axis=1)


def sweep_kernel(local_ref, i0, i1, i2, i3, ghost_ref, inv_ref, out_ref):
    count = local_ref.shape[0]
    hits = one_hot_rows(list_rows(ghost_ref[...])[:1], count)
    incoming = jnp.concatenate([i0[...], i1[...], i2[...], i3[...]], axis=0)
    rhs = local_ref[...] + jnp.dot(hits, incoming, preferred_element_type=f32)
    out_ref[...] = apply_blocks(inv_ref, rhs.astype(bf16)).astype(bf16)


def own_rows_kernel(
    coef_ref, fs_ref, nb_ref, ci_ref, face_ref, table_ref, hits_ref, own_ref, faces_ref, where_ref, scale_ref, w_ref
):
    count = fs_ref.shape[0]
    own, even_x, even_y = position()
    off = nb_ref[...] // count - own
    index_t = (nb_ref[...] % count).T
    block_t = jnp.where(off == 0, 0, 1 + partner(off, even_x, even_y)).T
    scale = jnp.zeros(off.shape, f32)
    for k in range(KINDS):
        scale = jnp.where(ci_ref[...] == k, coef_ref[k], scale)
    scale_t = scale.T
    for f in range(FACES):
        column = jnp.broadcast_to(index_t[:, f : f + 1], (count, LANES)).astype(i16)
        hits = one_hot_columns(column, count)
        rows = slice(f * count, (f + 1) * count)
        hits_ref[rows, :] = hits
        own_ref[rows, :] = jnp.dot(hits, fs_ref[...], preferred_element_type=f32).astype(bf16)
        faces_ref[f * W : (f + 1) * W, :] = block_diagonal(face_ref[f], True)
        where_ref[rows, :] = jnp.broadcast_to(block_t[:, f : f + 1], (count, LANES)).astype(i16)
        scale_ref[rows, :] = jnp.broadcast_to(scale_t[:, f : f + 1], (count, LANES))
    for t in range(NTYPE):
        w_ref[t * W : (t + 1) * W, :] = block_diagonal(table_ref[t], False)


def couple_kernel(
    fs_ref, h0, h1, h2, h3, hits_ref, own_ref, faces_ref, where_ref, scale_ref, ghost_ref, inv_ref,
    sol_ref, ans_ref, r0, r1, r2, r3,
):
    count = fs_ref.shape[0]
    coupled = jnp.zeros((count, W), f32)
    for f in range(FACES):
        rows = slice(f * count, (f + 1) * count)
        where = wide(where_ref[rows, :])
        beside = own_ref[rows, :]
        for q, source in enumerate((h0, h1, h2, h3)):
            found = jnp.dot(hits_ref[rows, :], source[...], preferred_element_type=f32).astype(bf16)
            beside = jnp.where(where == jnp.asarray(q + 1, i16), found, beside)
        term = jnp.dot(beside, faces_ref[f * W : (f + 1) * W, :], preferred_element_type=f32)
        coupled = coupled + term * wide(scale_ref[rows, :])
    correction = apply_blocks(inv_ref, coupled.astype(bf16))
    solution_rows = fs_ref[...].astype(f32) - OMEGA * correction
    sol_ref[...] = solution_rows
    answer = solution_rows.astype(bf16)
    ans_ref[...] = answer
    listed = jnp.broadcast_to(list_rows(ghost_ref[...]).T[:, :1], (4 * GHOST, LANES)).astype(i16)
    replies = jnp.dot(one_hot_columns(listed, count), answer, preferred_element_type=f32).astype(bf16)
    for q, out in enumerate((r0, r1, r2, r3)):
        out[...] = replies[q * GHOST : (q + 1) * GHOST, :]


def fetch_kernel(ans_ref, dest_ref, slot_ref, sol_ref, out_ref, sol_hbm, sem):
    store = pltpu.make_async_copy(sol_ref, sol_hbm, sem)
    store.start()
    count = ans_ref.shape[0]
    target = targets(dest_ref[...], slot_ref[...], count)
    for g in range(out_ref.shape[0] // CHUNK):
        column = columns(target[g * (CHUNK // LANES) : (g + 1) * (CHUNK // LANES), :])
        for r in range(0, CHUNK, PB):
            hits = one_hot_columns(column[r : r + PB, :], count)
            first = g * CHUNK + r
            out_ref[first : first + PB, :] = jnp.dot(hits, ans_ref[...], preferred_element_type=f32).astype(bf16)
    store.wait()


def prolong_kernel(count, local_ref, r0, r1, r2, r3, w_ref, dest_ref, slot_ref, type_ref, out_ref):
    step = pl.program_id(0)
    target = columns(targets(dest_ref[...], slot_ref[...], count) - count)
    returned = jnp.concatenate([r0[...], r1[...], r2[...], r3[...]], axis=0)
    remote = jnp.dot(one_hot_columns(target, 4 * GHOST), returned, preferred_element_type=f32)
    local = local_ref[pl.ds(pl.multiple_of(step * CHUNK, CHUNK), CHUNK), :]
    fetched = (local.astype(f32) + remote).astype(bf16)
    out_ref[...] = typed(fetched, columns(type_ref[...]), w_ref[...], PB)


VMEM = pl.BlockSpec(memory_space=pltpu.VMEM)


def in_hbm(x):
    return pltpu.with_memory_space_constraint(x, pltpu.HBM)


def ghost_shape():
    return [pltpu.VMEM((GHOST, W), bf16)] * 4


def whole(shape):
    return pl.BlockSpec(shape, lambda *_: (0,) * len(shape))


def restrict(x, meta, table, inverse):
    steps = x.shape[0] // CHUNK
    meta_spec = pl.BlockSpec((CHUNK // LANES, LANES), lambda i: (i, 0))
    return pl.pallas_call(
        restrict_kernel,
        grid=(steps,),
        in_specs=[pl.BlockSpec((CHUNK, W), lambda i: (i, 0)), meta_spec, meta_spec, meta_spec, whole(table.shape), pl.BlockSpec(memory_space=pltpu.HBM)],
        out_specs=[VMEM] * 6,
        out_shape=[pltpu.VMEM(x.shape, bf16)] + ghost_shape() + [pltpu.VMEM(inverse.shape, bf16)],
        scratch_shapes=[pltpu.VMEM((NTYPE * W, W), bf16), pltpu.VMEM((4 * GHOST, W), f32), pltpu.SemaphoreType.DMA],
        compiler_params=pltpu.CompilerParams(vmem_limit_bytes=VMEM_BYTES),
        name="restrict",
    )(x, *meta, table, inverse)


def local_sums(contrib, meta, count):
    return pl.pallas_call(
        local_kernel,
        in_specs=[VMEM] * 3,
        out_specs=VMEM,
        out_shape=pltpu.VMEM((count, W), f32),
        compiler_params=pltpu.CompilerParams(vmem_limit_bytes=VMEM_BYTES),
        name="local_sums",
    )(contrib, meta[0], meta[1])


def sweep(local, incoming, ghost, inverse):
    return pl.pallas_call(
        sweep_kernel,
        in_specs=[VMEM] * 7,
        out_specs=VMEM,
        out_shape=pltpu.VMEM(local.shape, bf16),
        compiler_params=pltpu.CompilerParams(vmem_limit_bytes=VMEM_BYTES),
        name="sweep",
    )(local, *incoming, ghost, inverse)


def own_rows(coef, first_sweep, neighbours, coef_index, face_table, table):
    count = first_sweep.shape[0]
    rows = FACES * count
    return pl.pallas_call(
        own_rows_kernel,
        in_specs=[pl.BlockSpec(memory_space=pltpu.SMEM)] + [VMEM] * 5,
        out_specs=[VMEM] * 6,
        out_shape=[
            pltpu.VMEM((rows, count), bf16), pltpu.VMEM((rows, W), bf16), pltpu.VMEM((FACES * W, W), bf16),
            pltpu.VMEM((rows, LANES), i16), pltpu.VMEM((rows, LANES), f32), pltpu.VMEM((NTYPE * W, W), bf16),
        ],
        compiler_params=pltpu.CompilerParams(vmem_limit_bytes=VMEM_BYTES),
        name="own_rows",
    )(coef, first_sweep, neighbours, coef_index, face_table, table)


def couple(first_sweep, halo, prepared, ghost, inverse):
    count = first_sweep.shape[0]
    return pl.pallas_call(
        couple_kernel,
        in_specs=[VMEM] * 12,
        out_specs=[VMEM] * 6,
        out_shape=[pltpu.VMEM((count, W), f32), pltpu.VMEM((count, W), bf16)] + ghost_shape(),
        compiler_params=pltpu.CompilerParams(vmem_limit_bytes=VMEM_BYTES),
        name="couple",
    )(first_sweep, *halo, *prepared, ghost, inverse)


def fetch(answer, meta, solution_rows):
    fine_count = meta[0].shape[0] * LANES
    return pl.pallas_call(
        fetch_kernel,
        in_specs=[VMEM] * 4,
        out_specs=[VMEM, pl.BlockSpec(memory_space=pltpu.HBM)],
        out_shape=[pltpu.VMEM((fine_count, W), bf16), jax.ShapeDtypeStruct(solution_rows.shape, f32)],
        scratch_shapes=[pltpu.SemaphoreType.DMA],
        compiler_params=pltpu.CompilerParams(vmem_limit_bytes=VMEM_BYTES),
        name="fetch",
    )(answer, meta[0], meta[1], solution_rows)


def prolong(local, returned, table, meta, count):
    fine_count = local.shape[0]
    meta_spec = pl.BlockSpec((CHUNK // LANES, LANES), lambda i: (i, 0))
    return pl.pallas_call(
        functools.partial(prolong_kernel, count),
        grid=(fine_count // CHUNK,),
        in_specs=[VMEM] * 6 + [meta_spec, meta_spec, meta_spec],
        out_specs=pl.BlockSpec((CHUNK, W), lambda i: (i, 0)),
        out_shape=jax.ShapeDtypeStruct((fine_count, W), bf16),
        compiler_params=pltpu.CompilerParams(vmem_limit_bytes=VMEM_BYTES),
        name="prolong",
    )(local, *returned, table, *meta)


def shards(
    fine_residual, dest_owner, coarse_slot, ghost_slot, child_type, restrict_table, inverse_blocks,
    face_table, face_coef, coef_index, neighbours,
):
    fine_count = fine_residual.shape[0]
    perms = swap_pairs(lax.axis_size("px"), lax.axis_size("py"))
    meta = [m.reshape(fine_count // LANES, LANES) for m in (dest_owner, coarse_slot, child_type)]
    contrib, *outgoing, inverse = restrict(
        in_hbm(fine_residual), [in_hbm(m) for m in meta], in_hbm(restrict_table), in_hbm(inverse_blocks)
    )
    incoming = exchange(outgoing, perms)
    local = local_sums(contrib, meta, inverse_blocks.shape[0])
    first_sweep = sweep(local, incoming, ghost_slot, inverse)
    halo = exchange([first_sweep] * 4, perms)
    *prepared, table = own_rows(
        face_coef, first_sweep, neighbours, coef_index, face_table, restrict_table
    )
    solution_rows, answer, *replies = couple(first_sweep, halo, prepared, ghost_slot, inverse)
    returned = exchange(replies, perms)
    fetched, coarse_solution = fetch(answer, meta, solution_rows)
    fine_correction = prolong(fetched, returned, table, meta, inverse_blocks.shape[0])
    return (coarse_solution, fine_correction)


def solution(mesh):
    both = ("px", "py")
    in_specs = (
        P(both, None), P(both), P(both), P(both, None), P(both), P(), P(both, None), P(), P(), P(None, both), P(None, both),
    )
    out_specs = (P(both, None), P(both, None))
    return jax.shard_map(shards, mesh=mesh, in_specs=in_specs, out_specs=out_specs, check_vma=False)
```

```python
import functools

import jax
import jax.numpy as jnp
from jax import lax
from jax.experimental import pallas as pl
from jax.experimental.pallas import tpu as pltpu
from jax.sharding import PartitionSpec as P


bf16 = jnp.bfloat16
f32 = jnp.float32
i32 = jnp.int32
i16 = jnp.int16

OMEGA = 0.5
DOF = 64
RHS = 4
W = 256
NTYPE = 8
FACES = 6
KINDS = 16
GHOST = 32
LANES = 128
CHUNK = 1024
RB = 128
PB = 512
VMEM_BYTES = 40 * 2**20


def swap_pairs(n_px, n_py):
    def at(a, b):
        return (a % n_px) * n_py + b % n_py

    perms = []
    for start in (0, 1):
        perm = []
        for b in range(n_py):
            for a in range(start, n_px + start, 2):
                perm += [(at(a, b), at(a + 1, b)), (at(a + 1, b), at(a, b))]
        perms.append(sorted(perm))
    for start in (0, 1):
        perm = []
        for a in range(n_px):
            for b in range(start, n_py + start, 2):
                perm += [(at(a, b), at(a, b + 1)), (at(a, b + 1), at(a, b))]
        perms.append(sorted(perm))
    return perms


def exchange(arrays, perms):
    moved = []
    for x, perm in zip(arrays, perms):
        moved.append(pltpu.with_memory_space_constraint(lax.ppermute(x, ("px", "py"), perm), pltpu.VMEM))
    return moved


def wide(column):
    return jnp.concatenate([column, column], axis=1)


def block_diagonal(matrix, flipped):
    row = lax.broadcasted_iota(i32, (W, DOF), 0) % DOF
    col = lax.broadcasted_iota(i32, (W, DOF), 1)
    spread = (row == col).astype(f32).astype(bf16)
    dims = (((1,), (1 if flipped else 0,)), ((), ()))
    half = lax.dot_general(spread, matrix, dims, preferred_element_type=f32).astype(bf16)
    full = lax.dot_general(half, spread, (((1,), (1,)), ((), ())), preferred_element_type=f32)
    r = lax.broadcasted_iota(i32, (W, W), 0) // DOF
    c = lax.broadcasted_iota(i32, (W, W), 1) // DOF
    return jnp.where(r == c, full, 0.0).astype(bf16)


def position():
    a, b = lax.axis_index("px"), lax.axis_index("py")
    n_py = lax.axis_size("py")
    return a * n_py + b, lax.rem(a, 2) == 0, lax.rem(b, 2) == 0


def partner(off, even_x, even_y):
    q_px = jnp.where((off > 0) == even_x, 0, 1)
    q_py = jnp.where((off > 0) == even_y, 2, 3)
    return jnp.where((off == 1) | (off == -1), q_py, q_px)


def targets(dest, slot, coarse_count):
    own, even_x, even_y = position()
    off = dest - own
    return jnp.where(off == 0, slot, coarse_count + partner(off, even_x, even_y) * GHOST + slot)


def list_rows(ghost):
    _, even_x, even_y = position()
    low_y, high_y, low_x, high_x = (ghost[j : j + 1, :] for j in range(4))
    ordered = [
        jnp.where(even_x, high_x, low_x),
        jnp.where(even_x, low_x, high_x),
        jnp.where(even_y, high_y, low_y),
        jnp.where(even_y, low_y, high_y),
    ]
    return jnp.broadcast_to(jnp.concatenate(ordered, axis=1), (8, 4 * GHOST))


def ones_where(mask):
    return jnp.where(mask, jnp.ones((), bf16), jnp.zeros((), bf16))


def one_hot_rows(values, row_count):
    row_id = lax.broadcasted_iota(i32, (row_count, LANES), 0).astype(i16)
    hits = []
    for r in range(values.shape[0]):
        wanted = jnp.broadcast_to(values[r : r + 1, :], (16, LANES)).astype(i16)
        wanted = jnp.concatenate([wanted] * (row_count // 16), axis=0)
        hits.append(ones_where(row_id == wanted))
    return jnp.concatenate(hits, axis=1)


def columns(rows):
    flipped = rows.T
    parts = [
        jnp.broadcast_to(flipped[:, r : r + 1], (LANES, LANES)).astype(i16) for r in range(rows.shape[0])
    ]
    return jnp.concatenate(parts, axis=0)


def one_hot_columns(column, row_count):
    lane = lax.broadcasted_iota(i32, column.shape, 1).astype(i16)
    return jnp.concatenate(
        [ones_where(column - jnp.asarray(k * LANES, i16) == lane) for k in range(row_count // LANES)], axis=1
    )


def typed(x_rows, kinds, table, rows):
    outs = []
    for r in range(0, x_rows.shape[0], rows):
        x, kind = x_rows[r : r + rows], kinds[r : r + rows]
        parts = [x * wide(ones_where(kind == jnp.asarray(t, i16))) for t in range(NTYPE)]
        outs.append(jnp.dot(jnp.concatenate(parts, axis=1), table, preferred_element_type=f32).astype(bf16))
    return jnp.concatenate(outs, axis=0)


def restrict_kernel(
    x_ref, dest_ref, slot_ref, type_ref, table_ref, inv_hbm, contrib_ref, g0, g1, g2, g3, inv_ref, w_ref, acc_ref, sem
):
    step = pl.program_id(0)
    coarse_count = inv_ref.shape[0]

    load = pltpu.make_async_copy(inv_hbm, inv_ref, sem)

    @pl.when(step == 0)
    def _():
        load.start()
        for t in range(NTYPE):
            w_ref[t * W : (t + 1) * W, :] = block_diagonal(table_ref[t], True)
        acc_ref[...] = jnp.zeros_like(acc_ref)

    contrib = typed(x_ref[...], columns(type_ref[...]), w_ref[...], RB)
    contrib_ref[pl.ds(pl.multiple_of(step * CHUNK, CHUNK), CHUNK), :] = contrib
    remote = targets(dest_ref[...], slot_ref[...], coarse_count) - coarse_count
    acc_ref[...] += jnp.dot(one_hot_rows(remote, 4 * GHOST), contrib, preferred_element_type=f32)

    @pl.when(step == pl.num_programs(0) - 1)
    def _():
        for q, out in enumerate((g0, g1, g2, g3)):
            out[...] = acc_ref[q * GHOST : (q + 1) * GHOST, :].astype(bf16)
        load.wait()


def local_kernel(contrib_ref, dest_ref, slot_ref, out_ref):
    count = out_ref.shape[0]
    target = targets(dest_ref[...], slot_ref[...], count)
    group = CHUNK // LANES
    total = jnp.zeros(out_ref.shape, f32)
    for g in range(contrib_ref.shape[0] // CHUNK):
        hits = one_hot_rows(target[g * group : (g + 1) * group, :], count)
        total = total + jnp.dot(hits, contrib_ref[g * CHUNK : (g + 1) * CHUNK, :], preferred_element_type=f32)
    out_ref[...] = total


def apply_blocks(inv_ref, v):
    count = v.shape[0]
    lane = lax.broadcasted_iota(i32, (count, LANES), 1)
    row = lax.broadcasted_iota(i32, (DOF * DOF, DOF), 0)
    col = lax.broadcasted_iota(i32, (DOF * DOF, DOF), 1)
    summing = (col == row // DOF).astype(f32).astype(bf16)
    outs = []
    for s in range(RHS):
        tile = v[:, (s // 2) * LANES : (s // 2 + 1) * LANES].astype(f32)
        turned = pltpu.roll(tile, DOF, 1)
        low, high = (tile, turned) if s % 2 == 0 else (turned, tile)
        doubled = jnp.where(lane < DOF, low, high).astype(bf16)
        products = jnp.concatenate(
            [inv_ref[:, k * LANES : (k + 1) * LANES] * doubled for k in range(DOF * DOF // LANES)], axis=1
        )
        outs.append(jnp.dot(products, summing, preferred_element_type=f32))
    return jnp.concatenate(outs, axis=1)


def sweep_kernel(local_ref, i0, i1, i2, i3, ghost_ref, inv_ref, out_ref):
    count = local_ref.shape[0]
    hits = one_hot_rows(list_rows(ghost_ref[...])[:1], count)
    incoming = jnp.concatenate([i0[...], i1[...], i2[...], i3[...]], axis=0)
    rhs = local_ref[...] + jnp.dot(hits, incoming, preferred_element_type=f32)
    out_ref[...] = apply_blocks(inv_ref, rhs.astype(bf16)).astype(bf16)


def own_rows_kernel(
    coef_ref, fs_ref, nb_ref, ci_ref, face_ref, table_ref, hits_ref, own_ref, faces_ref, where_ref, scale_ref, w_ref
):
    count = fs_ref.shape[0]
    own, even_x, even_y = position()
    off = nb_ref[...] // count - own
    index_t = (nb_ref[...] % count).T
    block_t = jnp.where(off == 0, 0, 1 + partner(off, even_x, even_y)).T
    scale = jnp.zeros(off.shape, f32)
    for k in range(KINDS):
        scale = jnp.where(ci_ref[...] == k, coef_ref[k], scale)
    scale_t = scale.T
    for f in range(FACES):
        column = jnp.broadcast_to(index_t[:, f : f + 1], (count, LANES)).astype(i16)
        hits = one_hot_columns(column, count)
        rows = slice(f * count, (f + 1) * count)
        hits_ref[rows, :] = hits
        own_ref[rows, :] = jnp.dot(hits, fs_ref[...], preferred_element_type=f32).astype(bf16)
        faces_ref[f * W : (f + 1) * W, :] = block_diagonal(face_ref[f], True)
        where_ref[rows, :] = jnp.broadcast_to(block_t[:, f : f + 1], (count, LANES)).astype(i16)
        scale_ref[rows, :] = jnp.broadcast_to(scale_t[:, f : f + 1], (count, LANES))
    for t in range(NTYPE):
        w_ref[t * W : (t + 1) * W, :] = block_diagonal(table_ref[t], False)


def couple_kernel(
    fs_ref, h0, h1, h2, h3, hits_ref, own_ref, faces_ref, where_ref, scale_ref, ghost_ref, inv_ref,
    sol_ref, ans_ref, r0, r1, r2, r3,
):
    count = fs_ref.shape[0]
    coupled = jnp.zeros((count, W), f32)
    for f in range(FACES):
        rows = slice(f * count, (f + 1) * count)
        where = wide(where_ref[rows, :])
        beside = own_ref[rows, :]
        for q, source in enumerate((h0, h1, h2, h3)):
            found = jnp.dot(hits_ref[rows, :], source[...], preferred_element_type=f32).astype(bf16)
            beside = jnp.where(where == jnp.asarray(q + 1, i16), found, beside)
        term = jnp.dot(beside, faces_ref[f * W : (f + 1) * W, :], preferred_element_type=f32)
        coupled = coupled + term * wide(scale_ref[rows, :])
    correction = apply_blocks(inv_ref, coupled.astype(bf16))
    solution_rows = fs_ref[...].astype(f32) - OMEGA * correction
    sol_ref[...] = solution_rows
    answer = solution_rows.astype(bf16)
    ans_ref[...] = answer
    listed = jnp.broadcast_to(list_rows(ghost_ref[...]).T[:, :1], (4 * GHOST, LANES)).astype(i16)
    replies = jnp.dot(one_hot_columns(listed, count), answer, preferred_element_type=f32).astype(bf16)
    for q, out in enumerate((r0, r1, r2, r3)):
        out[...] = replies[q * GHOST : (q + 1) * GHOST, :]


def fetch_kernel(ans_ref, dest_ref, slot_ref, sol_ref, out_ref, sol_hbm, sem):
    store = pltpu.make_async_copy(sol_ref, sol_hbm, sem)
    store.start()
    count = ans_ref.shape[0]
    target = targets(dest_ref[...], slot_ref[...], count)
    for g in range(out_ref.shape[0] // CHUNK):
        column = columns(target[g * (CHUNK // LANES) : (g + 1) * (CHUNK // LANES), :])
        for r in range(0, CHUNK, PB):
            hits = one_hot_columns(column[r : r + PB, :], count)
            first = g * CHUNK + r
            out_ref[first : first + PB, :] = jnp.dot(hits, ans_ref[...], preferred_element_type=f32).astype(bf16)
    store.wait()


def prolong_kernel(
    count, local_ref, r0, r1, r2, r3, w_ref, dest_ref, slot_ref, type_ref, out_hbm, out_ref, sems
):
    chunks = local_ref.shape[0] // CHUNK
    group = CHUNK // LANES
    returned = jnp.concatenate([r0[...], r1[...], r2[...], r3[...]], axis=0)

    def store_rows(k):
        rows = pl.ds(pl.multiple_of(k * PB, PB), PB)
        return pltpu.make_async_copy(out_ref.at[rows, :], out_hbm.at[rows, :], sems.at[k])

    def one_chunk(g, carry):
        lines = pl.ds(pl.multiple_of(g * group, group), group)
        target = columns(targets(dest_ref[lines, :], slot_ref[lines, :], count) - count)
        kinds = columns(type_ref[lines, :])
        for r in range(0, CHUNK, PB):
            rows = pl.ds(pl.multiple_of(g * CHUNK + r, PB), PB)
            remote = jnp.dot(one_hot_columns(target[r : r + PB], 4 * GHOST), returned, preferred_element_type=f32)
            fetched = (local_ref[rows, :].astype(f32) + remote).astype(bf16)
            out_ref[rows, :] = typed(fetched, kinds[r : r + PB], w_ref[...], PB)
            store_rows(g * (CHUNK // PB) + r // PB).start()
        return carry

    lax.fori_loop(0, chunks, one_chunk, 0, unroll=True)
    for k in range(local_ref.shape[0] // PB):
        store_rows(k).wait()


VMEM = pl.BlockSpec(memory_space=pltpu.VMEM)


def in_hbm(x):
    return pltpu.with_memory_space_constraint(x, pltpu.HBM)


def ghost_shape():
    return [pltpu.VMEM((GHOST, W), bf16)] * 4


def whole(shape):
    return pl.BlockSpec(shape, lambda *_: (0,) * len(shape))


def restrict(x, meta, table, inverse):
    steps = x.shape[0] // CHUNK
    meta_spec = pl.BlockSpec((CHUNK // LANES, LANES), lambda i: (i, 0))
    return pl.pallas_call(
        restrict_kernel,
        grid=(steps,),
        in_specs=[pl.BlockSpec((CHUNK, W), lambda i: (i, 0)), meta_spec, meta_spec, meta_spec, whole(table.shape), pl.BlockSpec(memory_space=pltpu.HBM)],
        out_specs=[VMEM] * 6,
        out_shape=[pltpu.VMEM(x.shape, bf16)] + ghost_shape() + [pltpu.VMEM(inverse.shape, bf16)],
        scratch_shapes=[pltpu.VMEM((NTYPE * W, W), bf16), pltpu.VMEM((4 * GHOST, W), f32), pltpu.SemaphoreType.DMA],
        compiler_params=pltpu.CompilerParams(vmem_limit_bytes=VMEM_BYTES),
        name="restrict",
    )(x, *meta, table, inverse)


def local_sums(contrib, meta, count):
    return pl.pallas_call(
        local_kernel,
        in_specs=[VMEM] * 3,
        out_specs=VMEM,
        out_shape=pltpu.VMEM((count, W), f32),
        compiler_params=pltpu.CompilerParams(vmem_limit_bytes=VMEM_BYTES),
        name="local_sums",
    )(contrib, meta[0], meta[1])


def sweep(local, incoming, ghost, inverse):
    return pl.pallas_call(
        sweep_kernel,
        in_specs=[VMEM] * 7,
        out_specs=VMEM,
        out_shape=pltpu.VMEM(local.shape, bf16),
        compiler_params=pltpu.CompilerParams(vmem_limit_bytes=VMEM_BYTES),
        name="sweep",
    )(local, *incoming, ghost, inverse)


def own_rows(coef, first_sweep, neighbours, coef_index, face_table, table):
    count = first_sweep.shape[0]
    rows = FACES * count
    return pl.pallas_call(
        own_rows_kernel,
        in_specs=[pl.BlockSpec(memory_space=pltpu.SMEM)] + [VMEM] * 5,
        out_specs=[VMEM] * 6,
        out_shape=[
            pltpu.VMEM((rows, count), bf16), pltpu.VMEM((rows, W), bf16), pltpu.VMEM((FACES * W, W), bf16),
            pltpu.VMEM((rows, LANES), i16), pltpu.VMEM((rows, LANES), f32), pltpu.VMEM((NTYPE * W, W), bf16),
        ],
        compiler_params=pltpu.CompilerParams(vmem_limit_bytes=VMEM_BYTES),
        name="own_rows",
    )(coef, first_sweep, neighbours, coef_index, face_table, table)


def couple(first_sweep, halo, prepared, ghost, inverse):
    count = first_sweep.shape[0]
    return pl.pallas_call(
        couple_kernel,
        in_specs=[VMEM] * 12,
        out_specs=[VMEM] * 6,
        out_shape=[pltpu.VMEM((count, W), f32), pltpu.VMEM((count, W), bf16)] + ghost_shape(),
        compiler_params=pltpu.CompilerParams(vmem_limit_bytes=VMEM_BYTES),
        name="couple",
    )(first_sweep, *halo, *prepared, ghost, inverse)


def fetch(answer, meta, solution_rows):
    fine_count = meta[0].shape[0] * LANES
    return pl.pallas_call(
        fetch_kernel,
        in_specs=[VMEM] * 4,
        out_specs=[VMEM, pl.BlockSpec(memory_space=pltpu.HBM)],
        out_shape=[pltpu.VMEM((fine_count, W), bf16), jax.ShapeDtypeStruct(solution_rows.shape, f32)],
        scratch_shapes=[pltpu.SemaphoreType.DMA],
        compiler_params=pltpu.CompilerParams(vmem_limit_bytes=VMEM_BYTES),
        name="fetch",
    )(answer, meta[0], meta[1], solution_rows)


def prolong(local, returned, table, meta, count):
    fine_count = local.shape[0]
    return pl.pallas_call(
        functools.partial(prolong_kernel, count),
        in_specs=[VMEM] * 9,
        out_specs=pl.BlockSpec(memory_space=pltpu.HBM),
        out_shape=jax.ShapeDtypeStruct((fine_count, W), bf16),
        scratch_shapes=[pltpu.VMEM((fine_count, W), bf16), pltpu.SemaphoreType.DMA((fine_count // PB,))],
        compiler_params=pltpu.CompilerParams(vmem_limit_bytes=VMEM_BYTES),
        name="prolong",
    )(local, *returned, table, *meta)


def shards(
    fine_residual, dest_owner, coarse_slot, ghost_slot, child_type, restrict_table, inverse_blocks,
    face_table, face_coef, coef_index, neighbours,
):
    fine_count = fine_residual.shape[0]
    perms = swap_pairs(lax.axis_size("px"), lax.axis_size("py"))
    meta = [m.reshape(fine_count // LANES, LANES) for m in (dest_owner, coarse_slot, child_type)]
    contrib, *outgoing, inverse = restrict(
        in_hbm(fine_residual), [in_hbm(m) for m in meta], in_hbm(restrict_table), in_hbm(inverse_blocks)
    )
    incoming = exchange(outgoing, perms)
    local = local_sums(contrib, meta, inverse_blocks.shape[0])
    first_sweep = sweep(local, incoming, ghost_slot, inverse)
    halo = exchange([first_sweep] * 4, perms)
    *prepared, table = own_rows(
        face_coef, first_sweep, neighbours, coef_index, face_table, restrict_table
    )
    solution_rows, answer, *replies = couple(first_sweep, halo, prepared, ghost_slot, inverse)
    returned = exchange(replies, perms)
    fetched, coarse_solution = fetch(answer, meta, solution_rows)
    fine_correction = prolong(fetched, returned, table, meta, inverse_blocks.shape[0])
    return (coarse_solution, fine_correction)


def solution(mesh):
    both = ("px", "py")
    in_specs = (
        P(both, None), P(both), P(both), P(both, None), P(both), P(), P(both, None), P(), P(), P(None, both), P(None, both),
    )
    out_specs = (P(both, None), P(both, None))
    return jax.shard_map(shards, mesh=mesh, in_specs=in_specs, out_specs=out_specs, check_vma=False)
```
